256 devices in a mesh: samp: 16 (over z, core), feat: 16 (over x, y).
Axes of the slice: x: 4, y: 4, z: 8, core: 2. Of those that a mesh axis runs over, the one named last changes fastest.
Arguments:
- differences: bfloat16 [9216, 131072], P('samp', 'feat'), may hold values from -600 to 600
- start_block: bfloat16 [64, 131072], P(None, 'feat'), may hold values from -6 to 6
Outputs:
- directions: float32 [64, 131072], P(None, 'feat')
- layer_scores: float32 [16, 64], P('feat')
The draws below stay inside these ranges and needn't reach their ends.
All inputs are finite; a program needn't handle non-finite values.
Results may differ from the reference program's by a relative error of at most 0.0043.
Values may be sent and summed in bfloat16 or wider, within the bound.
A program may use at most 64 MiB of HBM per device.

```python
import math
import jax
import jax.numpy as jnp
from jax import lax

WIDTH = 8192
LAYERS = 16
K = 64
ITERS = 2
NS = 9216
FEATURES = 131072


def draw_differences(key, part):
    keys = jax.random.split(key, 3)
    row_pos = jnp.arange(NS, dtype=jnp.float32) / NS
    col_pos = jnp.arange(FEATURES, dtype=jnp.float32) / FEATURES
    row_scale = (1.0 + 2.0 * row_pos) * jnp.exp(jax.random.uniform(keys[0], (NS,), jnp.float32) * jnp.log(10.0))
    col_scale = (1.0 + 2.0 * col_pos) * jnp.exp(jax.random.uniform(keys[1], (FEATURES,), jnp.float32) * jnp.log(10.0))
    noise = jnp.clip(jax.random.normal(keys[2], (NS, FEATURES), jnp.float32), -6.0, 6.0)
    values = 0.1 * noise * row_scale[:, None] * col_scale[None, :]
    return jnp.clip(values, -600.0, 600.0).astype(jnp.bfloat16)


def level_of(stream_key, dims, cuts, low, high):
    gain = 1.0
    for position, parts in cuts:
        draws = jax.random.uniform(jax.random.fold_in(jax.random.fold_in(stream_key, 6), position), (parts,), jnp.float32, low / len(cuts), high / len(cuts))
        gain = gain * jnp.repeat(jnp.exp(draws), dims[position] // parts).reshape((-1,) + (1,) * (len(dims) - 1 - position))
    return gain


def normal_values(stream_key, extent, spread, reach, pieces=(), kind=jnp.bfloat16):
    factor_of = level_of(stream_key, extent, pieces, -0.22, 0.18) if pieces else 1.0
    array = jax.random.normal(stream_key, extent, jnp.float32) * spread * factor_of
    return jnp.minimum(jnp.maximum(array, -reach), reach).astype(kind)


def setup_inputs(seed: int = 0) -> dict:
    splits = jax.random.split(jax.random.key(seed), 3)
    differences = draw_differences(jax.random.fold_in(splits[2], 71), 0)
    start_block = normal_values(splits[1], (K, FEATURES), 1.0, 6.0, ((1, 16),))
    return dict(differences=differences, start_block=start_block)


def reference(differences, start_block):
    block = start_block
    basis = None
    for step in range(ITERS):
        projected = jnp.dot(block.astype(jnp.float32), differences.T.astype(jnp.float32), preferred_element_type=jnp.float32).astype(jnp.bfloat16)
        pulled = jnp.dot(projected.astype(jnp.float32), differences.astype(jnp.float32), preferred_element_type=jnp.float32)
        gram = jnp.dot(pulled, pulled.T, precision=lax.Precision.HIGHEST)
        lower = jnp.linalg.cholesky(gram)
        basis = lax.linalg.triangular_solve(lower, pulled, left_side=True, lower=True)
        block = basis.astype(jnp.bfloat16)
    directions = basis * math.sqrt(FEATURES)
    score_rows = []
    for layer in range(LAYERS):
        piece = differences[:, layer * WIDTH:(layer + 1) * WIDTH]
        part = block[:, layer * WIDTH:(layer + 1) * WIDTH]
        along = jnp.dot(part.astype(jnp.float32), piece.T.astype(jnp.float32), preferred_element_type=jnp.float32)
        captured = lax.optimization_barrier(jnp.sum(along * along, axis=1))
        wide = piece.astype(jnp.float32)
        energy = jnp.sum(wide * wide)
        score_rows.append(FEATURES * captured / (energy + 1e-06))
    return (directions, jnp.stack(score_rows, axis=0))
```

```python
import functools
import math

import jax
import jax.numpy as jnp
from jax import lax
from jax.experimental import pallas as pl
from jax.experimental.pallas import tpu as pltpu
from jax.sharding import PartitionSpec as P

FEATURES = 131072
K = 64
NS = 576
WF = 8192
NP = 16
PW = WF // NP
HALF = PW // 2
ROWS = K // 16
WQ = NS + K
MESH = pl.DeviceIdType.MESH
F32 = jnp.float32
BF16 = jnp.bfloat16


def dot_nn(a, b):
    return lax.dot_general(a, b, (((1,), (0,)), ((), ())), preferred_element_type=F32)


def dot_nt(a, b):
    return lax.dot_general(a, b, (((1,), (1,)), ((), ())), preferred_element_type=F32)


def dot_exact(a, b):
    return lax.dot_general(a, b, (((1,), (0,)), ((), ())), preferred_element_type=F32, precision=lax.Precision.HIGHEST)


def inverse_factor(gram):
    row = lax.broadcasted_iota(jnp.int32, (K, K), 0)
    col = lax.broadcasted_iota(jnp.int32, (K, K), 1)
    m = jnp.concatenate([gram, jnp.where(row == col, 1.0, 0.0).astype(F32)], axis=1)
    below = lax.broadcasted_iota(jnp.int32, (K, 1), 0)
    scale = jnp.zeros((K, 1), F32)
    for j in range(K):
        pivot_row = m[j:j + 1, :]
        d = pivot_row[:, j:j + 1]
        scale = jnp.where(below == j, d, scale)
        if j < K - 1:
            factor = jnp.where(below > j, m[:, j:j + 1] * (1.0 / d), 0.0)
            m = m - factor * pivot_row
    inv = lax.rsqrt(scale)
    inv = inv * (1.5 - 0.5 * ((scale * inv) * inv))
    return m[:, K:] * inv


def kernel(d_hbm, s_hbm, dir_hbm, score_ref,
           dv, sv, x2, psend, precv, rs_s, rs_r, ls_s, ls_r, r0_s, r0_r, l0_s, l0_r, acc,
           qs, qr, qo, qg, qf, hs, hr, ho, hg, hf, fs, dout,
           d_sem, s_sem, o_sem, ar_s, ar_r, pair_s, pair_r, rr_s, rr_r, rl_s, rl_r,
           ag_rs, ag_rr, ag_ls, ag_lr, sib_s, sib_r, f_s, f_r):
    samp = lax.axis_index("samp")
    feat = lax.axis_index("feat")
    z = samp // 2
    c = samp % 2
    right = (((z + 1) % 8) * 2 + c, feat)
    left = (((z + 7) % 8) * 2 + c, feat)
    sibling = (z * 2 + (1 - c), feat)
    pending = []

    def send(src, dst, ssem, rsem, dev):
        copy = pltpu.make_async_remote_copy(src_ref=src, dst_ref=dst, send_sem=ssem, recv_sem=rsem,
                                            device_id=dev, device_id_type=MESH)
        copy.start()
        pending.append(copy)
        return copy

    barrier = pltpu.get_barrier_semaphore()
    for r in range(1, 16):
        pl.semaphore_signal(barrier, inc=1, device_id=(samp, (feat + r) % 16), device_id_type=MESH)
        pl.semaphore_signal(barrier, inc=1, device_id=((samp + r) % 16, feat), device_id_type=MESH)

    d_copies = []
    for p in range(NP):
        dc = pltpu.make_async_copy(d_hbm.at[:, p * PW:(p + 1) * PW], dv.at[p, 0:NS, :], d_sem.at[p])
        sc = pltpu.make_async_copy(s_hbm.at[:, p * PW:(p + 1) * PW], sv.at[p], s_sem.at[p])
        sc.start()
        dc.start()
        d_copies.append((dc, sc))

    def all_reduce(it, parts, arrived, own, gathered, full):
        copies = []
        for r in range(1, 16):
            copies.append(send(parts.at[(feat + r) % 16], arrived.at[r], ar_s.at[it, 0, r], ar_r.at[it, 0, r],
                               (samp, (feat + r) % 16)))
        yield
        total = parts[feat]
        for r in range(1, 16):
            copies[r - 1].wait_recv()
            total = total + arrived[r]
        own[...] = total
        copies = []
        for r in range(1, 16):
            copies.append(send(own, gathered.at[r], ar_s.at[it, 1, r], ar_r.at[it, 1, r],
                               (samp, (feat + r) % 16)))
        gathered[0] = total
        yield
        for r in range(1, 16):
            copies[r - 1].wait_recv()
        for j in range(16):
            full[j * ROWS:(j + 1) * ROWS, :] = gathered[(feat - j + 16) % 16]
        yield

    def split(value, parts):
        for j in range(16):
            parts[j] = value[j * ROWS:(j + 1) * ROWS, :]

    q = jnp.zeros((K, NS), F32)
    for p in range(NP):
        dc, sc = d_copies[p]
        sc.wait()
        dc.wait()
        q = q + dot_nt(sv[p], dv[p, 0:NS, :])
    split(jnp.concatenate([q, jnp.zeros((K, K), F32)], axis=1), qs.at[0])
    pl.semaphore_wait(barrier, 30)
    reduce = all_reduce(0, qs.at[0], qr.at[0], qo.at[0], qg.at[0], qf.at[0])
    next(reduce)

    def energy_step(p, total):
        wide = dv[p, 0:NS, :].astype(F32)
        return total + jnp.sum(wide * wide, axis=0, keepdims=True)

    energy = lax.fori_loop(0, NP, energy_step, jnp.zeros((1, PW), F32))
    energy = jnp.sum(energy, axis=1, keepdims=True)
    next(reduce)
    next(reduce)
    projected = qf[0, :, 0:NS].astype(BF16)

    def pull_and_scatter(it, projected):
        pair = {}

        def compute(d):
            there = (z + d) % 8
            psend[it, d] = dot_nn(projected, dv[(1 - c) * 8 + there, 0:NS, :]).astype(BF16)
            pair[d] = send(psend.at[it, d], precv.at[it, d], pair_s.at[it, d], pair_r.at[it, d], sibling)
            acc[d] = dot_nn(projected, dv[c * 8 + there, 0:NS, :])

        def both(d):
            pair[d].wait_recv()
            return acc[d] + precv[it, d].astype(F32)

        compute(4)
        compute(3)
        compute(5)
        far = both(4)
        r0_s[it] = far[:, 0:HALF].astype(BF16)
        l0_s[it] = far[:, HALF:].astype(BF16)
        to_right = send(r0_s.at[it], r0_r.at[it], rr_s.at[it, 0], rr_r.at[it, 0], right)
        to_left = send(l0_s.at[it], l0_r.at[it], rl_s.at[it, 0], rl_r.at[it, 0], left)
        compute(2)
        for t in range(1, 4):
            part = both(4 - t)
            to_right.wait_recv()
            if t == 1:
                rs_s[it, t, :, 0:HALF] = (part[:, 0:HALF] + r0_r[it].astype(F32)).astype(BF16)
                rs_s[it, t, :, HALF:] = part[:, HALF:].astype(BF16)
            else:
                rs_s[it, t] = (part + rs_r[it, t - 1].astype(F32)).astype(BF16)
            to_right = send(rs_s.at[it, t], rs_r.at[it, t], rr_s.at[it, t], rr_r.at[it, t], right)
            part = both(4 + t)
            to_left.wait_recv()
            if t == 1:
                ls_s[it, t, :, 0:HALF] = part[:, 0:HALF].astype(BF16)
                ls_s[it, t, :, HALF:] = (part[:, HALF:] + l0_r[it].astype(F32)).astype(BF16)
            else:
                ls_s[it, t] = (part + ls_r[it, t - 1].astype(F32)).astype(BF16)
            to_left = send(ls_s.at[it, t], ls_r.at[it, t], rl_s.at[it, t], rl_r.at[it, t], left)
            if t == 1:
                compute(6)
                compute(1)
            elif t == 2:
                compute(7)
                compute(0)
        part = both(0)
        to_right.wait_recv()
        to_left.wait_recv()
        return (part + rs_r[it, 3].astype(F32) + ls_r[it, 3].astype(F32)).astype(BF16)

    def gather(it, slot, use):
        here = c * 8
        there = (1 - c) * 8

        def to_sibling(d):
            p = here + (z + d) % 8
            return send(slot(p), slot(p), sib_s.at[it, d], sib_r.at[it, d], sibling)

        def ring(t, d, cols, sems, dev):
            p = here + (z + d) % 8
            src = slot(p) if cols is None else slot(p).at[:, cols]
            return send(src, src, sems[0].at[it, t], sems[1].at[it, t], dev)

        rsem = (ag_rs, ag_rr)
        lsem = (ag_ls, ag_lr)
        sib = {}
        to_right = ring(1, 0, None, rsem, right)
        to_left = ring(1, 0, None, lsem, left)
        sib[0] = to_sibling(0)
        use(here + z)
        for t in range(1, 4):
            nxt = None if t < 3 else True
            to_right.wait_recv()
            to_right = ring(t + 1, 8 - t, None if t < 3 else slice(0, HALF), rsem, right)
            sib[8 - t] = to_sibling(8 - t)
            to_left.wait_recv()
            to_left = ring(t + 1, t, None if t < 3 else slice(HALF, PW), lsem, left)
            sib[t] = to_sibling(t)
            if t == 1:
                sib[0].wait_recv()
                use(there + z)
            else:
                sib[9 - t].wait_recv()
                use(there + (z + 9 - t) % 8)
                sib[t - 1].wait_recv()
                use(there + (z + t - 1) % 8)
            use(here + (z + 8 - t) % 8)
            use(here + (z + t) % 8)
        to_right.wait_recv()
        to_left.wait_recv()
        sib[4] = to_sibling(4)
        use(here + (z + 4) % 8)
        sib[5].wait_recv()
        use(there + (z + 5) % 8)
        sib[3].wait_recv()
        use(there + (z + 3) % 8)
        sib[4].wait_recv()
        use(there + (z + 4) % 8)

    piece = pull_and_scatter(0, projected)
    dv[samp_piece(z, c), NS:, :] = piece
    qf[1] = jnp.zeros((K, WQ), F32)

    def use_first(p):
        qf[1] += dot_nt(dv[p, NS:, :], dv[p])

    gather(0, lambda p: dv.at[p, NS:, :], use_first)
    split(qf[1], qs.at[1])
    reduce = all_reduce(1, qs.at[1], qr.at[1], qo.at[1], qg.at[1], qf.at[2])
    next(reduce)
    next(reduce)
    next(reduce)
    inv = inverse_factor(qf[2, :, NS:])
    projected = dot_exact(inv, qf[2, :, 0:NS]).astype(BF16)

    piece = pull_and_scatter(1, projected)
    x2[samp_piece(z, c)] = piece
    qf[3] = jnp.zeros((K, WQ), F32)
    hf[0] = jnp.zeros((K, 128), F32)

    def use_second(p):
        x = x2[p]
        qf[3, :, 0:NS] += dot_nt(x, dv[p, 0:NS, :])
        hf[0, :, 0:K] += dot_nt(x, x)

    gather(1, lambda p: x2.at[p], use_second)
    split(hf[0], hs)
    reduce = all_reduce(2, hs, hr, ho, hg, hf.at[1])
    next(reduce)
    next(reduce)
    next(reduce)
    inv = inverse_factor(hf[1, :, 0:K])
    along = dot_exact(inv, qf[3, :, 0:NS])
    captured = lax.dot_general(jnp.ones((8, NS), F32), along * along, (((1,), (1,)), ((), ())),
                               preferred_element_type=F32, precision=lax.Precision.HIGHEST)
    fs[samp] = jnp.concatenate([captured, jnp.broadcast_to(energy, (8, K))], axis=1)
    last = []
    for r in range(1, 16):
        last.append(send(fs.at[samp], fs.at[samp], f_s.at[r], f_r.at[r], ((samp + r) % 16, feat)))

    scaled = inv * math.sqrt(FEATURES)
    high = scaled.astype(BF16)
    low = (scaled - high.astype(F32)).astype(BF16)
    stacked = jnp.concatenate([high, low], axis=0)
    outs = []
    for p in range(NP):
        both = dot_nn(stacked, x2[p])
        dout[p] = both[0:K] + both[K:]
        oc = pltpu.make_async_copy(dout.at[p], dir_hbm.at[:, p * PW:(p + 1) * PW], o_sem.at[p])
        oc.start()
        outs.append(oc)
    for copy in last:
        copy.wait_recv()
    total = fs[0]
    for r in range(1, 16):
        total = total + fs[r]
    score_ref[...] = FEATURES * total[:, 0:K] / (total[:, K:] + 1e-6)
    for oc in outs:
        oc.wait()
    for copy in pending:
        copy.wait_send()


def samp_piece(z, c):
    return c * 8 + z


def on_device(differences, start_block):
    dma = pltpu.SemaphoreType.DMA
    directions, scores = pl.pallas_call(
        kernel,
        out_shape=(jax.ShapeDtypeStruct((K, WF), F32), jax.ShapeDtypeStruct((8, K), F32)),
        in_specs=[pl.BlockSpec(memory_space=pl.ANY), pl.BlockSpec(memory_space=pl.ANY)],
        out_specs=(pl.BlockSpec(memory_space=pl.ANY), pl.BlockSpec(memory_space=pltpu.VMEM)),
        scratch_shapes=[
            pltpu.VMEM((NP, WQ, PW), BF16),
            pltpu.VMEM((NP, K, PW), BF16),
            pltpu.VMEM((NP, K, PW), BF16),
            pltpu.VMEM((2, 8, K, PW), BF16),
            pltpu.VMEM((2, 8, K, PW), BF16),
            pltpu.VMEM((2, 4, K, PW), BF16),
            pltpu.VMEM((2, 4, K, PW), BF16),
            pltpu.VMEM((2, 4, K, PW), BF16),
            pltpu.VMEM((2, 4, K, PW), BF16),
            pltpu.VMEM((2, K, HALF), BF16),
            pltpu.VMEM((2, K, HALF), BF16),
            pltpu.VMEM((2, K, HALF), BF16),
            pltpu.VMEM((2, K, HALF), BF16),
            pltpu.VMEM((8, K, PW), F32),
            pltpu.VMEM((2, 16, ROWS, WQ), F32),
            pltpu.VMEM((2, 16, ROWS, WQ), F32),
            pltpu.VMEM((2, ROWS, WQ), F32),
            pltpu.VMEM((2, 16, ROWS, WQ), F32),
            pltpu.VMEM((4, K, WQ), F32),
            pltpu.VMEM((16, ROWS, 128), F32),
            pltpu.VMEM((16, ROWS, 128), F32),
            pltpu.VMEM((ROWS, 128), F32),
            pltpu.VMEM((16, ROWS, 128), F32),
            pltpu.VMEM((2, K, 128), F32),
            pltpu.VMEM((16, 8, 128), F32),
            pltpu.VMEM((NP, K, PW), F32),
            dma((NP,)), dma((NP,)), dma((NP,)),
            dma((3, 2, 16)), dma((3, 2, 16)),
            dma((2, 8)), dma((2, 8)),
            dma((2, 4)), dma((2, 4)), dma((2, 4)), dma((2, 4)),
            dma((2, 5)), dma((2, 5)), dma((2, 5)), dma((2, 5)),
            dma((2, 8)), dma((2, 8)),
            dma((16,)), dma((16,)),
        ],
        compiler_params=pltpu.CompilerParams(collective_id=0, has_side_effects=True, vmem_limit_bytes=48 * 1024 * 1024),
    )(differences, start_block)
    return directions, scores[0:1]


def solution(mesh):
    in_specs = (P("samp", "feat"), P(None, "feat"))
    out_specs = (P(None, "feat"), P("feat", None))
    return jax.shard_map(
        on_device, mesh=mesh, in_specs=in_specs, out_specs=out_specs, check_vma=False
    )
```

```python
import math

import jax
import jax.numpy as jnp
from jax import lax
from jax.experimental import pallas as pl
from jax.experimental.pallas import tpu as pltpu
from jax.sharding import PartitionSpec as P

FEATURES = 131072
K = 64
NS = 576
WF = 8192
NP = 16
PW = WF // NP
HALF = PW // 2
ROWS = K // 16
WQ = NS + K
MESH = pl.DeviceIdType.MESH
F32 = jnp.float32
BF16 = jnp.bfloat16


def dot_nn(a, b):
    return lax.dot_general(a, b, (((1,), (0,)), ((), ())), preferred_element_type=F32)


def dot_nt(a, b):
    return lax.dot_general(a, b, (((1,), (1,)), ((), ())), preferred_element_type=F32)


def dot_exact(a, b):
    return lax.dot_general(a, b, (((1,), (0,)), ((), ())), preferred_element_type=F32, precision=lax.Precision.HIGHEST)


def inverse_factor(gram):
    row = lax.broadcasted_iota(jnp.int32, (8, 2 * K), 0)
    col = lax.broadcasted_iota(jnp.int32, (8, 2 * K), 1)
    wide = jnp.concatenate([gram, jnp.zeros((K, K), F32)], axis=1)
    m = [wide[8 * g:8 * g + 8, :] + jnp.where(col == row + (K + 8 * g), 1.0, 0.0) for g in range(8)]
    out = []
    for b in range(8):
        cols = [[jnp.broadcast_to(m[g][:, 8 * b + k:8 * b + k + 1], (8, 2 * K)) for k in range(8)] for g in range(b, 8)]
        diag = jnp.zeros((8, 2 * K), F32)
        for k in range(8):
            d = cols[0][k][k:k + 1, :]
            r = 1.0 / d
            diag = jnp.where(row == k, d, diag)
            pivot_row = m[b][k:k + 1, :] * r
            factor = [jnp.where(row > k, cols[0][k], 0.0)] + [cols[i][k] for i in range(1, 8 - b)]
            for i in range(8 - b):
                m[b + i] = m[b + i] - factor[i] * pivot_row
            for kk in range(k + 1, 8):
                t = cols[0][k][kk:kk + 1, :] * r
                for i in range(8 - b):
                    cols[i][kk] = cols[i][kk] - factor[i] * t
        inv = lax.rsqrt(diag)
        inv = inv * (1.5 - 0.5 * ((diag * inv) * inv))
        out.append((m[b] * inv)[:, K:])
    return jnp.concatenate(out, axis=0)


def pack(square):
    return jnp.concatenate([square[0:K // 2], square[K // 2:]], axis=1)


def unpack(wide):
    return jnp.concatenate([wide[:, 0:K], wide[:, K:]], axis=0)


def ring_hops(d, n):
    return min(d, n - d)


PLANE = sorted([(dx, dy) for dx in range(4) for dy in range(4) if dx or dy],
               key=lambda o: -(ring_hops(o[0], 4) + ring_hops(o[1], 4)))
COLUMN = [4, 3, 5, 2, 6, 1, 7]


def kernel(d_hbm, s_hbm, dir_hbm, score_ref,
           dv, sv, x2, psend, precv, msg_s, msg_r, half_s, half_r, acc,
           qs, qr, qo, qg, qf, gg, es, cs, cr, cg, dout,
           d_sem, s_sem, o_sem, ar_s, ar_r, pair_s, pair_r, rs_s, rs_r,
           ag_s, ag_r, sib_s, sib_r, g_s, g_r, e_s, e_r, c_s, c_r):
    samp = lax.axis_index("samp")
    feat = lax.axis_index("feat")
    z = samp // 2
    c = samp % 2
    x = feat // 4
    y = feat % 4
    sibling = (z * 2 + (1 - c), feat)
    pending = []

    def chip(d):
        return (((z + d) % 8) * 2 + c, feat)

    def across(dx, dy):
        return ((x + dx) % 4) * 4 + (y + dy) % 4

    def send(src, dst, ssem, rsem, dev):
        copy = pltpu.make_async_remote_copy(src_ref=src, dst_ref=dst, send_sem=ssem, recv_sem=rsem,
                                            device_id=dev, device_id_type=MESH)
        copy.start()
        pending.append(copy)
        return copy

    barrier = pltpu.get_barrier_semaphore()
    for r in range(1, 16):
        pl.semaphore_signal(barrier, inc=1, device_id=(samp, (feat + r) % 16), device_id_type=MESH)
        pl.semaphore_signal(barrier, inc=1, device_id=((samp + r) % 16, feat), device_id_type=MESH)

    d_copies = []
    for p in range(NP):
        dc = pltpu.make_async_copy(d_hbm.at[:, p * PW:(p + 1) * PW], dv.at[p, 0:NS, :], d_sem.at[p])
        sc = pltpu.make_async_copy(s_hbm.at[:, p * PW:(p + 1) * PW], sv.at[p], s_sem.at[p])
        sc.start()
        dc.start()
        d_copies.append((dc, sc))

    def reduce_scatter_q(it, value):
        for j in range(16):
            qs[it, j] = value[j * ROWS:(j + 1) * ROWS, :]
        copies = []
        for dx, dy in PLANE:
            r = dx * 4 + dy
            there = across(dx, dy)
            copies.append((r, send(qs.at[it, there], qr.at[it, r], ar_s.at[it, 0, r], ar_r.at[it, 0, r], (samp, there))))
        return copies

    def gather_q(it, copies):
        total = qs[it, feat]
        for r, copy in copies:
            copy.wait_recv()
            total = total + qr[it, r]
        qo[it] = total
        qg[it, 0] = total
        copies = []
        for dx, dy in PLANE:
            r = dx * 4 + dy
            copies.append(send(qo.at[it], qg.at[it, r], ar_s.at[it, 1, r], ar_r.at[it, 1, r], (samp, across(dx, dy))))
        return copies

    def join_q(it, copies):
        for copy in copies:
            copy.wait_recv()
        for j in range(16):
            slot = ((x - j // 4 + 4) % 4) * 4 + (y - j % 4 + 4) % 4
            qf[2 + it, j * ROWS:(j + 1) * ROWS, :] = qg[it, slot]
        return qf[2 + it, :, 0:NS]

    def exchange_gram(it, gram):
        gg[it, feat] = pack(gram)
        copies = []
        for dx, dy in PLANE:
            r = dx * 4 + dy
            copies.append(send(gg.at[it, feat], gg.at[it, feat], g_s.at[it, r], g_r.at[it, r], (samp, across(dx, dy))))
        return copies

    def join_gram(it, copies):
        for copy in copies:
            copy.wait_recv()
        total = gg[it, 0]
        for j in range(1, 16):
            total = total + gg[it, j]
        return unpack(total)

    q = jnp.zeros((K, NS), F32)
    for p in range(NP):
        dc, sc = d_copies[p]
        sc.wait()
        dc.wait()
        q = q + dot_nt(sv[p], dv[p, 0:NS, :])
    pl.semaphore_wait(barrier, 30)
    copies = reduce_scatter_q(0, jnp.concatenate([q, jnp.zeros((K, K), F32)], axis=1))

    def energy_step(p, total):
        wide = dv[p, 0:NS, :].astype(F32)
        return total + jnp.sum(wide * wide, axis=0, keepdims=True)

    energy = lax.fori_loop(0, NP, energy_step, jnp.zeros((1, PW), F32))
    es[samp] = jnp.broadcast_to(jnp.sum(energy, axis=1, keepdims=True), (8, 128))
    copies = gather_q(0, copies)
    energy_copies = []
    for r in range(1, 16):
        energy_copies.append(send(es.at[samp], es.at[samp], e_s.at[r], e_r.at[r], ((samp + r) % 16, feat)))
    projected = join_q(0, copies).astype(BF16)

    def pull_and_scatter(it, projected):
        pair = {}

        def compute(d):
            there = (z + d) % 8
            psend[it, d] = dot_nn(projected, dv[(1 - c) * 8 + there, 0:NS, :]).astype(BF16)
            pair[d] = send(psend.at[it, d], precv.at[it, d], pair_s.at[it, d], pair_r.at[it, d], sibling)
            acc[d] = dot_nn(projected, dv[c * 8 + there, 0:NS, :])

        def both(d):
            pair[d].wait_recv()
            return acc[d] + precv[it, d].astype(F32)

        def post(slot, value, dev):
            msg_s[it, slot] = value.astype(BF16)
            return send(msg_s.at[it, slot], msg_r.at[it, slot], rs_s.at[it, slot], rs_r.at[it, slot], dev)

        def post_half(slot, value, dev):
            half_s[it, slot] = value.astype(BF16)
            return send(half_s.at[it, slot], half_r.at[it, slot], rs_s.at[it, 6 + slot], rs_r.at[it, 6 + slot], dev)

        compute(4)
        compute(3)
        compute(5)
        compute(2)
        part = both(4)
        far_r = post_half(0, part[:, 0:HALF], chip(2))
        far_l = post_half(1, part[:, HALF:], chip(6))
        mid_r = post(0, both(3), chip(1))
        mid_l = post(1, both(5), chip(7))
        compute(6)
        compute(1)
        compute(7)
        near_r = post(2, both(1), chip(1))
        near_l = post(3, both(7), chip(7))
        compute(0)
        acc[2] = both(2)
        acc[6] = both(6)
        mid_r.wait_recv()
        far_r.wait_recv()
        part = acc[2] + msg_r[it, 0].astype(F32)
        half = half_r[it, 0].astype(F32)
        sum_r = post(4, jnp.concatenate([part[:, 0:HALF] + half, part[:, HALF:]], axis=1), chip(2))
        mid_l.wait_recv()
        far_l.wait_recv()
        part = acc[6] + msg_r[it, 1].astype(F32)
        half = half_r[it, 1].astype(F32)
        sum_l = post(5, jnp.concatenate([part[:, 0:HALF], part[:, HALF:] + half], axis=1), chip(6))
        part = both(0)
        near_r.wait_recv()
        near_l.wait_recv()
        part = part + msg_r[it, 2].astype(F32) + msg_r[it, 3].astype(F32)
        sum_r.wait_recv()
        sum_l.wait_recv()
        return (part + msg_r[it, 4].astype(F32) + msg_r[it, 5].astype(F32)).astype(BF16)

    def gather(it, slot, use):
        here = c * 8
        there = (1 - c) * 8
        sib = {}

        def pass_on(k, d, dev, cols=None):
            p = here + (z + d) % 8
            ref = slot(p) if cols is None else slot(p).at[:, cols]
            return send(ref, ref, ag_s.at[it, k], ag_r.at[it, k], dev)

        def to_sibling(d):
            p = here + (z + d) % 8
            sib[d] = send(slot(p), slot(p), sib_s.at[it, d], sib_r.at[it, d], sibling)

        def use_sibling(d):
            sib[d].wait_recv()
            use(there + (z + d) % 8)

        two_r = pass_on(0, 0, chip(2))
        two_l = pass_on(1, 0, chip(6))
        one_r = pass_on(2, 0, chip(1))
        one_l = pass_on(3, 0, chip(7))
        to_sibling(0)
        use(here + z)
        use_sibling(0)
        one_r.wait_recv()
        to_sibling(7)
        one_l.wait_recv()
        to_sibling(1)
        two_r.wait_recv()
        four_r = pass_on(4, 6, chip(2), slice(0, HALF))
        three_r = pass_on(6, 6, chip(1))
        to_sibling(6)
        two_l.wait_recv()
        four_l = pass_on(5, 2, chip(6), slice(HALF, PW))
        three_l = pass_on(7, 2, chip(7))
        to_sibling(2)
        for d in (7, 1, 6, 2):
            use(here + (z + d) % 8)
        for d in (7, 1, 6, 2):
            use_sibling(d)
        three_r.wait_recv()
        to_sibling(5)
        three_l.wait_recv()
        to_sibling(3)
        use(here + (z + 5) % 8)
        use(here + (z + 3) % 8)
        four_r.wait_recv()
        four_l.wait_recv()
        to_sibling(4)
        use(here + (z + 4) % 8)
        use_sibling(5)
        use_sibling(3)
        use_sibling(4)

    piece = pull_and_scatter(0, projected)
    dv[c * 8 + z, NS:, :] = piece
    qf[0] = jnp.zeros((K, WQ), F32)

    def use_first(p):
        qf[0] += dot_nt(dv[p, NS:, :], dv[p])

    gather(0, lambda p: dv.at[p, NS:, :], use_first)
    copies = reduce_scatter_q(1, qf[0])
    gram_copies = exchange_gram(0, qf[0, :, NS:])
    copies = gather_q(1, copies)
    inv = inverse_factor(join_gram(0, gram_copies))
    projected = dot_exact(inv, join_q(1, copies)).astype(BF16)

    piece = pull_and_scatter(1, projected)
    x2[c * 8 + z] = piece
    qf[1] = jnp.zeros((K, WQ), F32)

    def use_second(p):
        block = x2[p]
        qf[1, :, 0:NS] += dot_nt(block, dv[p, 0:NS, :])
        acc[0, :, 0:K] += dot_nt(block, block)

    acc[0] = jnp.zeros((K, PW), F32)
    gather(1, lambda p: x2.at[p], use_second)
    gram_copies = exchange_gram(1, acc[0, :, 0:K])

    along = qf[1, :, 0:NS]
    cs[...] = pack(lax.dot_general(along, along, (((1,), (1,)), ((), ())), preferred_element_type=F32,
                                   precision=lax.Precision.HIGHEST))
    copy = send(cs, cr, c_s.at[0], c_r.at[0], sibling)
    copy.wait_recv()
    cg[z] = cs[...] + cr[...]
    c_copies = []
    for d in COLUMN:
        c_copies.append(send(cg.at[z], cg.at[z], c_s.at[d], c_r.at[d], chip(d)))
    inv = inverse_factor(join_gram(1, gram_copies))

    scaled = inv * math.sqrt(FEATURES)
    high = scaled.astype(BF16)
    low = (scaled - high.astype(F32)).astype(BF16)
    stacked = jnp.concatenate([high, low], axis=0)
    outs = []
    for p in range(NP):
        two = dot_nn(stacked, x2[p])
        dout[p] = two[0:K] + two[K:]
        oc = pltpu.make_async_copy(dout.at[p], dir_hbm.at[:, p * PW:(p + 1) * PW], o_sem.at[p])
        oc.start()
        outs.append(oc)
    for copy in energy_copies:
        copy.wait_recv()
    energy = es[0]
    for r in range(1, 16):
        energy = energy + es[r]
    for copy in c_copies:
        copy.wait_recv()
    total = cg[0]
    for d in range(1, 8):
        total = total + cg[d]
    spread = dot_exact(inv, unpack(total)) * inv
    captured = lax.dot_general(jnp.ones((8, K), F32), spread, (((1,), (1,)), ((), ())),
                               preferred_element_type=F32, precision=lax.Precision.HIGHEST)
    score_ref[...] = FEATURES * captured[0:1, :] / (energy[0:1, 0:K] + 1e-6)
    for oc in outs:
        oc.wait()
    for copy in pending:
        copy.wait_send()


def on_device(differences, start_block):
    dma = pltpu.SemaphoreType.DMA
    return pl.pallas_call(
        kernel,
        out_shape=(jax.ShapeDtypeStruct((K, WF), F32), jax.ShapeDtypeStruct((1, K), F32)),
        in_specs=[pl.BlockSpec(memory_space=pltpu.HBM), pl.BlockSpec(memory_space=pltpu.HBM)],
        out_specs=(pl.BlockSpec(memory_space=pltpu.HBM), pl.BlockSpec(memory_space=pltpu.VMEM)),
        scratch_shapes=[
            pltpu.VMEM((NP, WQ, PW), BF16),
            pltpu.VMEM((NP, K, PW), BF16),
            pltpu.VMEM((NP, K, PW), BF16),
            pltpu.VMEM((2, 8, K, PW), BF16),
            pltpu.VMEM((2, 8, K, PW), BF16),
            pltpu.VMEM((2, 6, K, PW), BF16),
            pltpu.VMEM((2, 6, K, PW), BF16),
            pltpu.VMEM((2, 2, K, HALF), BF16),
            pltpu.VMEM((2, 2, K, HALF), BF16),
            pltpu.VMEM((8, K, PW), F32),
            pltpu.VMEM((2, 16, ROWS, WQ), F32),
            pltpu.VMEM((2, 16, ROWS, WQ), F32),
            pltpu.VMEM((2, ROWS, WQ), F32),
            pltpu.VMEM((2, 16, ROWS, WQ), F32),
            pltpu.VMEM((4, K, WQ), F32),
            pltpu.VMEM((2, 16, K // 2, 128), F32),
            pltpu.VMEM((16, 8, 128), F32),
            pltpu.VMEM((K // 2, 128), F32),
            pltpu.VMEM((K // 2, 128), F32),
            pltpu.VMEM((8, K // 2, 128), F32),
            pltpu.VMEM((NP, K, PW), F32),
            dma((NP,)), dma((NP,)), dma((NP,)),
            dma((2, 2, 16)), dma((2, 2, 16)),
            dma((2, 8)), dma((2, 8)),
            dma((2, 8)), dma((2, 8)),
            dma((2, 8)), dma((2, 8)),
            dma((2, 8)), dma((2, 8)),
            dma((2, 16)), dma((2, 16)),
            dma((16,)), dma((16,)),
            dma((8,)), dma((8,)),
        ],
        compiler_params=pltpu.CompilerParams(collective_id=0, has_side_effects=True, vmem_limit_bytes=56 * 1024 * 1024),
    )(differences, start_block)


def solution(mesh):
    in_specs = (P("samp", "feat"), P(None, "feat"))
    out_specs = (P(None, "feat"), P("feat", None))
    return jax.shard_map(
        on_device, mesh=mesh, in_specs=in_specs, out_specs=out_specs, check_vma=False
    )
```

```python
import math

import jax
import jax.numpy as jnp
from jax import lax
from jax.experimental import pallas as pl
from jax.experimental.pallas import tpu as pltpu
from jax.sharding import PartitionSpec as P

FEATURES = 131072
K = 64
NS = 576
WF = 8192
NP = 16
PW = WF // NP
CHUNKS = 2
CW = PW // CHUNKS
HALF = CW // 2
ROWS = K // 16
WQ = NS + K
MESH = pl.DeviceIdType.MESH
F32 = jnp.float32
BF16 = jnp.bfloat16


def dot_nn(a, b):
    return lax.dot_general(a, b, (((1,), (0,)), ((), ())), preferred_element_type=F32)


def dot_nt(a, b):
    return lax.dot_general(a, b, (((1,), (1,)), ((), ())), preferred_element_type=F32)


def dot_exact(a, b):
    return lax.dot_general(a, b, (((1,), (0,)), ((), ())), preferred_element_type=F32, precision=lax.Precision.HIGHEST)


def inverse_factor(gram):
    row = lax.broadcasted_iota(jnp.int32, (8, 2 * K), 0)
    col = lax.broadcasted_iota(jnp.int32, (8, 2 * K), 1)
    wide = jnp.concatenate([gram, jnp.zeros((K, K), F32)], axis=1)
    m = [wide[8 * g:8 * g + 8, :] + jnp.where(col == row + (K + 8 * g), 1.0, 0.0) for g in range(8)]
    out = []
    for b in range(8):
        cols = [[jnp.broadcast_to(m[g][:, 8 * b + k:8 * b + k + 1], (8, 2 * K)) for k in range(8)] for g in range(b, 8)]
        diag = jnp.zeros((8, 2 * K), F32)
        for k in range(8):
            d = cols[0][k][k:k + 1, :]
            r = 1.0 / d
            diag = jnp.where(row == k, d, diag)
            pivot_row = m[b][k:k + 1, :] * r
            factor = [jnp.where(row > k, cols[0][k], 0.0)] + [cols[i][k] for i in range(1, 8 - b)]
            for i in range(8 - b):
                m[b + i] = m[b + i] - factor[i] * pivot_row
            for kk in range(k + 1, 8):
                t = cols[0][k][kk:kk + 1, :] * r
                for i in range(8 - b):
                    cols[i][kk] = cols[i][kk] - factor[i] * t
        inv = lax.rsqrt(diag)
        inv = inv * (1.5 - 0.5 * ((diag * inv) * inv))
        out.append((m[b] * inv)[:, K:])
    return jnp.concatenate(out, axis=0)


def pack(square):
    return jnp.concatenate([square[0:K // 2], square[K // 2:]], axis=1)


def unpack(wide):
    return jnp.concatenate([wide[:, 0:K], wide[:, K:]], axis=0)


def ring_hops(d, n):
    return min(d, n - d)


PLANE = sorted([(dx, dy) for dx in range(4) for dy in range(4) if dx or dy],
               key=lambda o: -(ring_hops(o[0], 4) + ring_hops(o[1], 4)))
COLUMN = [4, 3, 5, 2, 6, 1, 7]


def kernel(d_hbm, s_hbm, x2_out, factor_ref, score_ref,
           dv, sv, x2, psend, precv, msg_s, msg_r, half_s, half_r, acc,
           qs, qr, qo, qg, qf, gg, es, cs, cr, cg, g2,
           d_sem, s_sem, o_sem, ar_s, ar_r, pair_s, pair_r, rs_s, rs_r,
           ag_s, ag_r, sib_s, sib_r, g_s, g_r, e_s, e_r, c_s, c_r):
    samp = lax.axis_index("samp")
    feat = lax.axis_index("feat")
    z = samp // 2
    c = samp % 2
    x = feat // 4
    y = feat % 4
    sibling = (z * 2 + (1 - c), feat)
    pending = []

    def chip(d):
        return (((z + d) % 8) * 2 + c, feat)

    def across(dx, dy):
        return ((x + dx) % 4) * 4 + (y + dy) % 4

    def send(src, dst, ssem, rsem, dev):
        copy = pltpu.make_async_remote_copy(src_ref=src, dst_ref=dst, send_sem=ssem, recv_sem=rsem,
                                            device_id=dev, device_id_type=MESH)
        copy.start()
        pending.append(copy)
        return copy

    barrier = pltpu.get_barrier_semaphore()
    for r in range(1, 16):
        pl.semaphore_signal(barrier, inc=1, device_id=(samp, (feat + r) % 16), device_id_type=MESH)
        pl.semaphore_signal(barrier, inc=1, device_id=((samp + r) % 16, feat), device_id_type=MESH)

    d_copies = []
    for p in range(NP):
        dc = pltpu.make_async_copy(d_hbm.at[:, p * PW:(p + 1) * PW], dv.at[p, 0:NS, :], d_sem.at[p])
        sc = pltpu.make_async_copy(s_hbm.at[:, p * PW:(p + 1) * PW], sv.at[p], s_sem.at[p])
        sc.start()
        dc.start()
        d_copies.append((dc, sc))

    def reduce_scatter_q(it, value):
        for j in range(16):
            qs[it, j] = value[j * ROWS:(j + 1) * ROWS, :]
        copies = []
        for dx, dy in PLANE:
            r = dx * 4 + dy
            there = across(dx, dy)
            copies.append((r, send(qs.at[it, there], qr.at[it, r], ar_s.at[it, 0, r], ar_r.at[it, 0, r], (samp, there))))
        return copies

    def gather_q(it, copies):
        total = qs[it, feat]
        for r, copy in copies:
            copy.wait_recv()
            total = total + qr[it, r]
        qo[it] = total
        qg[it, 0] = total
        copies = []
        for dx, dy in PLANE:
            r = dx * 4 + dy
            copies.append(send(qo.at[it], qg.at[it, r], ar_s.at[it, 1, r], ar_r.at[it, 1, r], (samp, across(dx, dy))))
        return copies

    def join_q(it, copies):
        for copy in copies:
            copy.wait_recv()
        for j in range(16):
            slot = ((x - j // 4 + 4) % 4) * 4 + (y - j % 4 + 4) % 4
            qf[2 + it, j * ROWS:(j + 1) * ROWS, :] = qg[it, slot]
        return qf[2 + it, :, 0:NS]

    def exchange_gram(it, gram):
        gg[it, feat] = pack(gram)
        copies = []
        for dx, dy in PLANE:
            r = dx * 4 + dy
            copies.append(send(gg.at[it, feat], gg.at[it, feat], g_s.at[it, r], g_r.at[it, r], (samp, across(dx, dy))))
        return copies

    def join_gram(it, copies):
        for copy in copies:
            copy.wait_recv()
        total = gg[it, 0]
        for j in range(1, 16):
            total = total + gg[it, j]
        return unpack(total)

    q = jnp.zeros((K, NS), F32)
    for p in range(NP):
        dc, sc = d_copies[p]
        sc.wait()
        dc.wait()
        q = q + dot_nt(sv[p], dv[p, 0:NS, :])
    pl.semaphore_wait(barrier, 30)
    copies = reduce_scatter_q(0, jnp.concatenate([q, jnp.zeros((K, K), F32)], axis=1))

    def energy_step(p, total):
        wide = dv[p, 0:NS, :].astype(F32)
        return total + jnp.sum(wide * wide, axis=0, keepdims=True)

    energy = lax.fori_loop(0, NP, energy_step, jnp.zeros((1, PW), F32))
    es[samp] = jnp.broadcast_to(jnp.sum(energy, axis=1, keepdims=True), (8, 128))
    copies = gather_q(0, copies)
    energy_copies = []
    for r in range(1, 16):
        energy_copies.append(send(es.at[samp], es.at[samp], e_s.at[r], e_r.at[r], ((samp + r) % 16, feat)))
    projected = join_q(0, copies).astype(BF16)

    def pull_and_scatter(it, projected):
        pair = {}

        def compute(d):
            there = (z + d) % 8
            psend[it, d] = dot_nn(projected, dv[(1 - c) * 8 + there, 0:NS, :]).astype(BF16)
            pair[d] = send(psend.at[it, d], precv.at[it, d], pair_s.at[it, d], pair_r.at[it, d], sibling)
            acc[d] = dot_nn(projected, dv[c * 8 + there, 0:NS, :])

        def both(d):
            pair[d].wait_recv()
            return acc[d] + precv[it, d].astype(F32)

        def post(slot, ch, value, dev):
            msg_s[it, ch, slot] = value.astype(BF16)
            return send(msg_s.at[it, ch, slot], msg_r.at[it, ch, slot], rs_s.at[it, ch, slot], rs_r.at[it, ch, slot], dev)

        def post_half(slot, ch, value, dev):
            half_s[it, ch, slot] = value.astype(BF16)
            return send(half_s.at[it, ch, slot], half_r.at[it, ch, slot],
                        rs_s.at[it, ch, 6 + slot], rs_r.at[it, ch, 6 + slot], dev)

        def cols(ch):
            return slice(ch * CW, (ch + 1) * CW)

        compute(4)
        compute(3)
        compute(5)
        compute(2)
        part4, part3, part5 = both(4), both(3), both(5)
        far_r, far_l, mid_r, mid_l, near_r, near_l, sum_r, sum_l = [[None] * CHUNKS for _ in range(8)]
        for ch in range(CHUNKS):
            part = part4[:, cols(ch)]
            far_r[ch] = post_half(0, ch, part[:, 0:HALF], chip(2))
            far_l[ch] = post_half(1, ch, part[:, HALF:], chip(6))
            mid_r[ch] = post(0, ch, part3[:, cols(ch)], chip(1))
            mid_l[ch] = post(1, ch, part5[:, cols(ch)], chip(7))
        compute(6)
        compute(1)
        compute(7)
        part1, part7 = both(1), both(7)
        for ch in range(CHUNKS):
            near_r[ch] = post(2, ch, part1[:, cols(ch)], chip(1))
            near_l[ch] = post(3, ch, part7[:, cols(ch)], chip(7))
        compute(0)
        acc[2] = both(2)
        acc[6] = both(6)
        for ch in range(CHUNKS):
            mid_r[ch].wait_recv()
            far_r[ch].wait_recv()
            part = acc[2, :, cols(ch)] + msg_r[it, ch, 0].astype(F32)
            half = half_r[it, ch, 0].astype(F32)
            sum_r[ch] = post(4, ch, jnp.concatenate([part[:, 0:HALF] + half, part[:, HALF:]], axis=1), chip(2))
            mid_l[ch].wait_recv()
            far_l[ch].wait_recv()
            part = acc[6, :, cols(ch)] + msg_r[it, ch, 1].astype(F32)
            half = half_r[it, ch, 1].astype(F32)
            sum_l[ch] = post(5, ch, jnp.concatenate([part[:, 0:HALF], part[:, HALF:] + half], axis=1), chip(6))
        acc[0] = both(0)
        for ch in range(CHUNKS):
            near_r[ch].wait_recv()
            near_l[ch].wait_recv()
            part = acc[0, :, cols(ch)] + msg_r[it, ch, 2].astype(F32) + msg_r[it, ch, 3].astype(F32)
            sum_r[ch].wait_recv()
            sum_l[ch].wait_recv()
            yield (part + msg_r[it, ch, 4].astype(F32) + msg_r[it, ch, 5].astype(F32)).astype(BF16)

    def gather(it, slot, pieces, use):
        here = c * 8
        there = (1 - c) * 8
        sib = {}
        two_r, two_l, one_r, one_l, four_r, four_l, three_r, three_l = [[None] * CHUNKS for _ in range(8)]

        def pass_on(k, ch, d, dev, start=0, width=CW):
            ref = slot(here + (z + d) % 8, slice(ch * CW + start, ch * CW + start + width))
            return send(ref, ref, ag_s.at[it, ch, k], ag_r.at[it, ch, k], dev)

        def to_sibling(ch, d):
            ref = slot(here + (z + d) % 8, slice(ch * CW, (ch + 1) * CW))
            sib[ch, d] = send(ref, ref, sib_s.at[it, ch, d], sib_r.at[it, ch, d], sibling)

        def use_own(ch, d):
            use(here + (z + d) % 8, slice(ch * CW, (ch + 1) * CW))

        def use_sibling(ch, d):
            sib[ch, d].wait_recv()
            use(there + (z + d) % 8, slice(ch * CW, (ch + 1) * CW))

        for ch, piece in enumerate(pieces):
            slot(here + z, slice(ch * CW, (ch + 1) * CW))[...] = piece
            two_r[ch] = pass_on(0, ch, 0, chip(2))
            two_l[ch] = pass_on(1, ch, 0, chip(6))
            one_r[ch] = pass_on(2, ch, 0, chip(1))
            one_l[ch] = pass_on(3, ch, 0, chip(7))
            to_sibling(ch, 0)
        for ch in range(CHUNKS):
            use_own(ch, 0)
        for ch in range(CHUNKS):
            use_sibling(ch, 0)
        for ch in range(CHUNKS):
            one_r[ch].wait_recv()
            to_sibling(ch, 7)
            one_l[ch].wait_recv()
            to_sibling(ch, 1)
            two_r[ch].wait_recv()
            four_r[ch] = pass_on(4, ch, 6, chip(2), 0, HALF)
            three_r[ch] = pass_on(6, ch, 6, chip(1))
            to_sibling(ch, 6)
            two_l[ch].wait_recv()
            four_l[ch] = pass_on(5, ch, 2, chip(6), HALF, HALF)
            three_l[ch] = pass_on(7, ch, 2, chip(7))
            to_sibling(ch, 2)
            for d in (7, 1):
                use_own(ch, d)
        for ch in range(CHUNKS):
            for d in (6, 2):
                use_own(ch, d)
            for d in (7, 1, 6, 2):
                use_sibling(ch, d)
        for ch in range(CHUNKS):
            three_r[ch].wait_recv()
            to_sibling(ch, 5)
            three_l[ch].wait_recv()
            to_sibling(ch, 3)
            four_r[ch].wait_recv()
            four_l[ch].wait_recv()
            to_sibling(ch, 4)
            for d in (5, 3, 4):
                use_own(ch, d)
        for ch in range(CHUNKS):
            for d in (5, 3, 4):
                use_sibling(ch, d)

    qf[0] = jnp.zeros((K, WQ), F32)

    def use_first(p, cols):
        qf[0] += dot_nt(dv[p, NS:, cols], dv[p, :, cols])

    gather(0, lambda p, cols: dv.at[p, NS:, cols], pull_and_scatter(0, projected), use_first)
    copies = reduce_scatter_q(1, qf[0])
    gram_copies = exchange_gram(0, qf[0, :, NS:])
    copies = gather_q(1, copies)
    inv = inverse_factor(join_gram(0, gram_copies))
    projected = dot_exact(inv, join_q(1, copies)).astype(BF16)

    qf[1] = jnp.zeros((K, WQ), F32)

    g2[...] = jnp.zeros((K, K), F32)

    def use_second(p, cols):
        block = x2[p, :, cols]
        qf[1, :, 0:NS] += dot_nt(block, dv[p, 0:NS, cols])
        g2[...] += dot_nt(block, block)

    gather(1, lambda p, cols: x2.at[p, :, cols], pull_and_scatter(1, projected), use_second)
    gram_copies = exchange_gram(1, g2[...])
    out_copy = pltpu.make_async_copy(x2, x2_out, o_sem)
    out_copy.start()

    along = qf[1, :, 0:NS]
    cs[...] = pack(lax.dot_general(along, along, (((1,), (1,)), ((), ())), preferred_element_type=F32,
                                   precision=lax.Precision.HIGHEST))
    copy = send(cs, cr, c_s.at[0], c_r.at[0], sibling)
    copy.wait_recv()
    cg[z] = cs[...] + cr[...]
    c_copies = []
    for d in COLUMN:
        c_copies.append(send(cg.at[z], cg.at[z], c_s.at[d], c_r.at[d], chip(d)))
    inv = inverse_factor(join_gram(1, gram_copies))

    scaled = inv * math.sqrt(FEATURES)
    high = scaled.astype(BF16)
    low = (scaled - high.astype(F32)).astype(BF16)
    factor_ref[...] = jnp.concatenate([high, low], axis=0)
    for copy in energy_copies:
        copy.wait_recv()
    energy = es[0]
    for r in range(1, 16):
        energy = energy + es[r]
    for copy in c_copies:
        copy.wait_recv()
    total = cg[0]
    for d in range(1, 8):
        total = total + cg[d]
    spread = dot_exact(inv, unpack(total)) * inv
    captured = lax.dot_general(jnp.ones((8, K), F32), spread, (((1,), (1,)), ((), ())),
                               preferred_element_type=F32, precision=lax.Precision.HIGHEST)
    score_ref[...] = FEATURES * captured[0:1, :] / (energy[0:1, 0:K] + 1e-6)
    out_copy.wait()
    for copy in pending:
        copy.wait_send()


def write_directions(pulled_ref, factor_ref, score_in, dir_ref, score_ref):
    score_ref[...] = score_in[...]
    for i in range(pulled_ref.shape[0]):
        two = dot_nn(factor_ref[...], pulled_ref[i])
        dir_ref[:, i * PW:(i + 1) * PW] = two[0:K] + two[K:]


def on_device(differences, start_block):
    dma = pltpu.SemaphoreType.DMA
    pulled, factor, scores = pl.pallas_call(
        kernel,
        out_shape=(jax.ShapeDtypeStruct((NP, K, PW), BF16), jax.ShapeDtypeStruct((2 * K, K), BF16),
                   jax.ShapeDtypeStruct((1, K), F32)),
        in_specs=[pl.BlockSpec(memory_space=pltpu.HBM), pl.BlockSpec(memory_space=pltpu.HBM)],
        out_specs=(pl.BlockSpec(memory_space=pltpu.HBM), pl.BlockSpec(memory_space=pltpu.VMEM),
                   pl.BlockSpec(memory_space=pltpu.VMEM)),
        scratch_shapes=[
            pltpu.VMEM((NP, WQ, PW), BF16),
            pltpu.VMEM((NP, K, PW), BF16),
            pltpu.VMEM((NP, K, PW), BF16),
            pltpu.VMEM((2, 8, K, PW), BF16),
            pltpu.VMEM((2, 8, K, PW), BF16),
            pltpu.VMEM((2, CHUNKS, 6, K, CW), BF16),
            pltpu.VMEM((2, CHUNKS, 6, K, CW), BF16),
            pltpu.VMEM((2, CHUNKS, 2, K, HALF), BF16),
            pltpu.VMEM((2, CHUNKS, 2, K, HALF), BF16),
            pltpu.VMEM((8, K, PW), F32),
            pltpu.VMEM((2, 16, ROWS, WQ), F32),
            pltpu.VMEM((2, 16, ROWS, WQ), F32),
            pltpu.VMEM((2, ROWS, WQ), F32),
            pltpu.VMEM((2, 16, ROWS, WQ), F32),
            pltpu.VMEM((4, K, WQ), F32),
            pltpu.VMEM((2, 16, K // 2, 128), F32),
            pltpu.VMEM((16, 8, 128), F32),
            pltpu.VMEM((K // 2, 128), F32),
            pltpu.VMEM((K // 2, 128), F32),
            pltpu.VMEM((8, K // 2, 128), F32),
            pltpu.VMEM((K, K), F32),
            dma((NP,)), dma((NP,)), dma,
            dma((2, 2, 16)), dma((2, 2, 16)),
            dma((2, 8)), dma((2, 8)),
            dma((2, CHUNKS, 8)), dma((2, CHUNKS, 8)),
            dma((2, CHUNKS, 8)), dma((2, CHUNKS, 8)),
            dma((2, CHUNKS, 8)), dma((2, CHUNKS, 8)),
            dma((2, 16)), dma((2, 16)),
            dma((16,)), dma((16,)),
            dma((8,)), dma((8,)),
        ],
        compiler_params=pltpu.CompilerParams(collective_id=0, has_side_effects=True, vmem_limit_bytes=56 * 1024 * 1024),
    )(differences, start_block)
    step = 4
    return pl.pallas_call(
        write_directions,
        grid=(NP // step,),
        out_shape=(jax.ShapeDtypeStruct((K, WF), F32), jax.ShapeDtypeStruct((1, K), F32)),
        in_specs=[pl.BlockSpec((step, K, PW), lambda i: (i, 0, 0)), pl.BlockSpec((2 * K, K), lambda i: (0, 0)),
                  pl.BlockSpec((1, K), lambda i: (0, 0))],
        out_specs=(pl.BlockSpec((K, step * PW), lambda i: (0, i)), pl.BlockSpec((1, K), lambda i: (0, 0))),
    )(pulled, factor, scores)


def solution(mesh):
    in_specs = (P("samp", "feat"), P(None, "feat"))
    out_specs = (P(None, "feat"), P("feat", None))
    return jax.shard_map(
        on_device, mesh=mesh, in_specs=in_specs, out_specs=out_specs, check_vma=False
    )
```

```python
import math

import jax
import jax.numpy as jnp
from jax import lax
from jax.experimental import pallas as pl
from jax.experimental.pallas import tpu as pltpu
from jax.sharding import PartitionSpec as P

FEATURES = 131072
K = 64
NS = 576
WF = 8192
NP = 16
PW = WF // NP
CHUNKS = 2
CW = PW // CHUNKS
HALF = CW // 2
ROWS = K // 16
WQ = NS + K
GROUPS = 8
MESH = pl.DeviceIdType.MESH
F32 = jnp.float32
BF16 = jnp.bfloat16


def dot_nn(a, b):
    return lax.dot_general(a, b, (((1,), (0,)), ((), ())), preferred_element_type=F32)


def dot_nt(a, b):
    return lax.dot_general(a, b, (((1,), (1,)), ((), ())), preferred_element_type=F32)


def dot_exact(a, b):
    return lax.dot_general(a, b, (((1,), (0,)), ((), ())), preferred_element_type=F32, precision=lax.Precision.HIGHEST)


def inverse_factor(gram):
    row = lax.broadcasted_iota(jnp.int32, (8, 2 * K), 0)
    col = lax.broadcasted_iota(jnp.int32, (8, 2 * K), 1)
    wide = jnp.concatenate([gram, jnp.zeros((K, K), F32)], axis=1)
    m = [wide[8 * g:8 * g + 8, :] + jnp.where(col == row + (K + 8 * g), 1.0, 0.0) for g in range(8)]
    out = []
    for b in range(8):
        cols = [[jnp.broadcast_to(m[g][:, 8 * b + k:8 * b + k + 1], (8, 2 * K)) for k in range(8)] for g in range(b, 8)]
        diag = jnp.zeros((8, 2 * K), F32)
        for k in range(8):
            d = cols[0][k][k:k + 1, :]
            r = 1.0 / d
            diag = jnp.where(row == k, d, diag)
            pivot_row = m[b][k:k + 1, :] * r
            factor = [jnp.where(row > k, cols[0][k], 0.0)] + [cols[i][k] for i in range(1, 8 - b)]
            for i in range(8 - b):
                m[b + i] = m[b + i] - factor[i] * pivot_row
            for kk in range(k + 1, 8):
                t = cols[0][k][kk:kk + 1, :] * r
                for i in range(8 - b):
                    cols[i][kk] = cols[i][kk] - factor[i] * t
        inv = lax.rsqrt(diag)
        inv = inv * (1.5 - 0.5 * ((diag * inv) * inv))
        out.append((m[b] * inv)[:, K:])
    return jnp.concatenate(out, axis=0)


def pack(square):
    return jnp.concatenate([square[0:K // 2], square[K // 2:]], axis=1)


def unpack(wide):
    return jnp.concatenate([wide[:, 0:K], wide[:, K:]], axis=0)


def ring_hops(d, n):
    return min(d, n - d)


PLANE = sorted([(dx, dy) for dx in range(4) for dy in range(4) if dx or dy],
               key=lambda o: -(ring_hops(o[0], 4) + ring_hops(o[1], 4)))
COLUMN = [4, 3, 5, 2, 6, 1, 7]


def kernel(d_hbm, s_hbm, x2_out, factor_ref, score_ref,
           dv, sv, x2, psend, precv, msg_s, msg_r, half_s, half_r, acc,
           qs, qr, qo, qg, qf, gg, es, cs, cr, cg, g2,
           d_sem, s_sem, o_sem, ar_s, ar_r, pair_s, pair_r, rs_s, rs_r,
           ag_s, ag_r, sib_s, sib_r, g_s, g_r, e_s, e_r, c_s, c_r):
    samp = lax.axis_index("samp")
    feat = lax.axis_index("feat")
    z = samp // 2
    c = samp % 2
    x = feat // 4
    y = feat % 4
    sibling = (z * 2 + (1 - c), feat)
    pending = []

    def chip(d):
        return (((z + d) % 8) * 2 + c, feat)

    def across(dx, dy):
        return ((x + dx) % 4) * 4 + (y + dy) % 4

    def send(src, dst, ssem, rsem, dev):
        copy = pltpu.make_async_remote_copy(src_ref=src, dst_ref=dst, send_sem=ssem, recv_sem=rsem,
                                            device_id=dev, device_id_type=MESH)
        copy.start()
        pending.append(copy)
        return copy

    def flush(keep=0):
        while len(pending) > keep:
            pending.pop(0).wait_send()

    barrier = pltpu.get_barrier_semaphore()
    for r in range(1, 16):
        pl.semaphore_signal(barrier, inc=1, device_id=(samp, (feat + r) % 16), device_id_type=MESH)
        pl.semaphore_signal(barrier, inc=1, device_id=((samp + r) % 16, feat), device_id_type=MESH)

    d_copies = []
    for p in range(NP):
        dc = pltpu.make_async_copy(d_hbm.at[:, p * PW:(p + 1) * PW], dv.at[p, 0:NS, :], d_sem.at[p])
        sc = pltpu.make_async_copy(s_hbm.at[:, p * PW:(p + 1) * PW], sv.at[p], s_sem.at[p])
        sc.start()
        dc.start()
        d_copies.append((dc, sc))

    def reduce_scatter_q(it, value):
        for j in range(16):
            qs[it, j] = value[j * ROWS:(j + 1) * ROWS, :]
        copies = []
        for dx, dy in PLANE:
            r = dx * 4 + dy
            there = across(dx, dy)
            copies.append((r, send(qs.at[it, there], qr.at[it, r], ar_s.at[it, 0, r], ar_r.at[it, 0, r], (samp, there))))
        return copies

    def gather_q(it, copies):
        total = qs[it, feat]
        for r, copy in copies:
            copy.wait_recv()
            total = total + qr[it, r]
        qo[it] = total
        qg[it, 0] = total
        copies = []
        for dx, dy in PLANE:
            r = dx * 4 + dy
            copies.append(send(qo.at[it], qg.at[it, r], ar_s.at[it, 1, r], ar_r.at[it, 1, r], (samp, across(dx, dy))))
        flush(15)
        return copies

    def join_q(it, copies):
        for copy in copies:
            copy.wait_recv()
        for j in range(16):
            slot = ((x - j // 4 + 4) % 4) * 4 + (y - j % 4 + 4) % 4
            qf[2 + it, j * ROWS:(j + 1) * ROWS, :] = qg[it, slot]
        return qf[2 + it, :, 0:NS]

    def exchange_gram(it, gram):
        gg[it, feat] = pack(gram)
        copies = []
        for dx, dy in PLANE:
            r = dx * 4 + dy
            copies.append(send(gg.at[it, feat], gg.at[it, feat], g_s.at[it, r], g_r.at[it, r], (samp, across(dx, dy))))
        return copies

    def join_gram(it, copies):
        for copy in copies:
            copy.wait_recv()
        total = gg[it, 0]
        for j in range(1, 16):
            total = total + gg[it, j]
        return unpack(total)

    q = jnp.zeros((K, NS), F32)
    for p in range(NP):
        dc, sc = d_copies[p]
        sc.wait()
        dc.wait()
        q = q + dot_nt(sv[p], dv[p, 0:NS, :])
    pl.semaphore_wait(barrier, 30)
    copies = reduce_scatter_q(0, jnp.concatenate([q, jnp.zeros((K, K), F32)], axis=1))

    def energy_step(p, total):
        wide = dv[p, 0:NS, :].astype(F32)
        return total + jnp.sum(wide * wide, axis=0, keepdims=True)

    energy = lax.fori_loop(0, NP, energy_step, jnp.zeros((1, PW), F32))
    es[samp] = jnp.broadcast_to(jnp.sum(energy, axis=1, keepdims=True), (8, 128))
    copies = gather_q(0, copies)
    energy_copies = []
    for r in range(1, 16):
        energy_copies.append(send(es.at[samp], es.at[samp], e_s.at[r], e_r.at[r], ((samp + r) % 16, feat)))
    projected = join_q(0, copies).astype(BF16)

    def pull_and_scatter(it, projected):
        pair = {}

        def compute(d):
            there = (z + d) % 8
            psend[it, d] = dot_nn(projected, dv[(1 - c) * 8 + there, 0:NS, :]).astype(BF16)
            pair[d] = send(psend.at[it, d], precv.at[it, d], pair_s.at[it, d], pair_r.at[it, d], sibling)
            acc[d] = dot_nn(projected, dv[c * 8 + there, 0:NS, :])

        def both(d):
            pair[d].wait_recv()
            return acc[d] + precv[it, d].astype(F32)

        def post(slot, ch, value, dev):
            msg_s[it, ch, slot] = value.astype(BF16)
            return send(msg_s.at[it, ch, slot], msg_r.at[it, ch, slot], rs_s.at[it, ch, slot], rs_r.at[it, ch, slot], dev)

        def post_half(slot, ch, value, dev):
            half_s[it, ch, slot] = value.astype(BF16)
            return send(half_s.at[it, ch, slot], half_r.at[it, ch, slot],
                        rs_s.at[it, ch, 6 + slot], rs_r.at[it, ch, 6 + slot], dev)

        def cols(ch):
            return slice(ch * CW, (ch + 1) * CW)

        compute(4)
        compute(3)
        compute(5)
        compute(2)
        part4, part3, part5 = both(4), both(3), both(5)
        far_r, far_l, mid_r, mid_l, near_r, near_l, sum_r, sum_l = [[None] * CHUNKS for _ in range(8)]
        for ch in range(CHUNKS):
            part = part4[:, cols(ch)]
            far_r[ch] = post_half(0, ch, part[:, 0:HALF], chip(2))
            far_l[ch] = post_half(1, ch, part[:, HALF:], chip(6))
            mid_r[ch] = post(0, ch, part3[:, cols(ch)], chip(1))
            mid_l[ch] = post(1, ch, part5[:, cols(ch)], chip(7))
        compute(6)
        compute(1)
        compute(7)
        part1, part7 = both(1), both(7)
        for ch in range(CHUNKS):
            near_r[ch] = post(2, ch, part1[:, cols(ch)], chip(1))
            near_l[ch] = post(3, ch, part7[:, cols(ch)], chip(7))
        compute(0)
        acc[2] = both(2)
        acc[6] = both(6)
        for ch in range(CHUNKS):
            mid_r[ch].wait_recv()
            far_r[ch].wait_recv()
            part = acc[2, :, cols(ch)] + msg_r[it, ch, 0].astype(F32)
            half = half_r[it, ch, 0].astype(F32)
            sum_r[ch] = post(4, ch, jnp.concatenate([part[:, 0:HALF] + half, part[:, HALF:]], axis=1), chip(2))
            mid_l[ch].wait_recv()
            far_l[ch].wait_recv()
            part = acc[6, :, cols(ch)] + msg_r[it, ch, 1].astype(F32)
            half = half_r[it, ch, 1].astype(F32)
            sum_l[ch] = post(5, ch, jnp.concatenate([part[:, 0:HALF], part[:, HALF:] + half], axis=1), chip(6))
        acc[0] = both(0)
        for ch in range(CHUNKS):
            near_r[ch].wait_recv()
            near_l[ch].wait_recv()
            part = acc[0, :, cols(ch)] + msg_r[it, ch, 2].astype(F32) + msg_r[it, ch, 3].astype(F32)
            sum_r[ch].wait_recv()
            sum_l[ch].wait_recv()
            yield (part + msg_r[it, ch, 4].astype(F32) + msg_r[it, ch, 5].astype(F32)).astype(BF16)

    def gather(it, slot, pieces, use):
        here = c * 8
        there = (1 - c) * 8
        sib = {}
        two_r, two_l, one_r, one_l, four_r, four_l, three_r, three_l = [[None] * CHUNKS for _ in range(8)]

        def pass_on(k, ch, d, dev, start=0, width=CW):
            ref = slot(here + (z + d) % 8, slice(ch * CW + start, ch * CW + start + width))
            return send(ref, ref, ag_s.at[it, ch, k], ag_r.at[it, ch, k], dev)

        def to_sibling(ch, d):
            ref = slot(here + (z + d) % 8, slice(ch * CW, (ch + 1) * CW))
            sib[ch, d] = send(ref, ref, sib_s.at[it, ch, d], sib_r.at[it, ch, d], sibling)

        def use_own(ch, *ds):
            use([here + (z + d) % 8 for d in ds], slice(ch * CW, (ch + 1) * CW))

        def use_sibling(ch, *ds):
            for d in ds:
                sib[ch, d].wait_recv()
            use([there + (z + d) % 8 for d in ds], slice(ch * CW, (ch + 1) * CW))

        for ch, piece in enumerate(pieces):
            slot(here + z, slice(ch * CW, (ch + 1) * CW))[...] = piece
            two_r[ch] = pass_on(0, ch, 0, chip(2))
            two_l[ch] = pass_on(1, ch, 0, chip(6))
            to_sibling(ch, 0)
        for ch in range(CHUNKS):
            one_r[ch] = pass_on(2, ch, 0, chip(1))
            one_l[ch] = pass_on(3, ch, 0, chip(7))
        use_own(0, 0)
        use_own(1, 0)
        use_sibling(0, 0)
        use_sibling(1, 0)
        flush(10)
        for ch in range(CHUNKS):
            two_r[ch].wait_recv()
            four_r[ch] = pass_on(4, ch, 6, chip(2), 0, HALF)
            three_r[ch] = pass_on(6, ch, 6, chip(1))
            to_sibling(ch, 6)
            two_l[ch].wait_recv()
            four_l[ch] = pass_on(5, ch, 2, chip(6), HALF, HALF)
            three_l[ch] = pass_on(7, ch, 2, chip(7))
            to_sibling(ch, 2)
            use_own(ch, 6, 2)
        for ch in range(CHUNKS):
            one_r[ch].wait_recv()
            to_sibling(ch, 7)
            one_l[ch].wait_recv()
            to_sibling(ch, 1)
            use_own(ch, 7, 1)
            use_sibling(ch, 6, 2)
        use_sibling(0, 7, 1)
        use_sibling(1, 7, 1)
        for ch in range(CHUNKS):
            three_r[ch].wait_recv()
            to_sibling(ch, 5)
            three_l[ch].wait_recv()
            to_sibling(ch, 3)
            four_r[ch].wait_recv()
            four_l[ch].wait_recv()
            to_sibling(ch, 4)
            use_own(ch, 5, 3, 4)
        for ch in range(CHUNKS):
            use_sibling(ch, 5, 3, 4)

    qf[0] = jnp.zeros((K, WQ), F32)

    def use_first(ps, cols):
        qf[0] += sum(dot_nt(dv[p, NS:, cols], dv[p, :, cols]) for p in ps)

    gather(0, lambda p, cols: dv.at[p, NS:, cols], pull_and_scatter(0, projected), use_first)
    copies = reduce_scatter_q(1, qf[0])
    gram_copies = exchange_gram(0, qf[0, :, NS:])
    copies = gather_q(1, copies)
    inv = inverse_factor(join_gram(0, gram_copies))
    projected = dot_exact(inv, join_q(1, copies)).astype(BF16)

    qf[1] = jnp.zeros((K, WQ), F32)

    g2[...] = jnp.zeros((K, K), F32)

    def use_second(ps, cols):
        qf[1, :, 0:NS] += sum(dot_nt(x2[p, :, cols], dv[p, 0:NS, cols]) for p in ps)
        g2[...] += sum(dot_nt(x2[p, :, cols], x2[p, :, cols]) for p in ps)

    gather(1, lambda p, cols: x2.at[p, :, cols], pull_and_scatter(1, projected), use_second)
    gram_copies = exchange_gram(1, g2[...])
    out_copy = pltpu.make_async_copy(x2, x2_out, o_sem)
    out_copy.start()

    along = qf[1, :, 0:NS]
    cs[...] = pack(lax.dot_general(along, along, (((1,), (1,)), ((), ())), preferred_element_type=F32,
                                   precision=lax.Precision.HIGHEST))
    copy = send(cs, cr, c_s.at[0], c_r.at[0], sibling)
    copy.wait_recv()
    cg[z] = cs[...] + cr[...]
    c_copies = []
    for d in COLUMN:
        c_copies.append(send(cg.at[z], cg.at[z], c_s.at[d], c_r.at[d], chip(d)))
    flush(7)
    inv = inverse_factor(join_gram(1, gram_copies))

    scaled = inv * math.sqrt(FEATURES)
    high = scaled.astype(BF16)
    low = (scaled - high.astype(F32)).astype(BF16)
    factor_ref[...] = jnp.concatenate([high, low], axis=0)
    for copy in energy_copies:
        copy.wait_recv()
    energy = es[0]
    for r in range(1, 16):
        energy = energy + es[r]
    for copy in c_copies:
        copy.wait_recv()
    total = cg[0]
    for d in range(1, 8):
        total = total + cg[d]
    spread = dot_exact(inv, unpack(total)) * inv
    captured = lax.dot_general(jnp.ones((8, K), F32), spread, (((1,), (1,)), ((), ())),
                               preferred_element_type=F32, precision=lax.Precision.HIGHEST)
    score_ref[...] = FEATURES * captured[0:1, :] / (energy[0:1, 0:K] + 1e-6)
    out_copy.wait()
    flush()


def write_directions(pulled_ref, factor_ref, score_in, dir_ref, score_ref, here, out, in_sem, out_sem):
    reads = []
    for g in range(GROUPS):
        part = pl.ds(g * (NP // GROUPS), NP // GROUPS)
        reads.append(pltpu.make_async_copy(pulled_ref.at[part], here.at[part], in_sem.at[g]))
        reads[g].start()
    score_ref[...] = score_in[...]
    writes = []
    for g in range(GROUPS):
        reads[g].wait()
        for p in range(g * (NP // GROUPS), (g + 1) * (NP // GROUPS)):
            two = dot_nn(factor_ref[...], here[p])
            out[:, p * PW:(p + 1) * PW] = two[0:K] + two[K:]
        cols = pl.ds(g * (WF // GROUPS), WF // GROUPS)
        writes.append(pltpu.make_async_copy(out.at[:, cols], dir_ref.at[:, cols], out_sem.at[g]))
        writes[g].start()
    for copy in writes:
        copy.wait()


def on_device(differences, start_block):
    dma = pltpu.SemaphoreType.DMA
    pulled, factor, scores = pl.pallas_call(
        kernel,
        out_shape=(jax.ShapeDtypeStruct((NP, K, PW), BF16), jax.ShapeDtypeStruct((2 * K, K), BF16),
                   jax.ShapeDtypeStruct((1, K), F32)),
        in_specs=[pl.BlockSpec(memory_space=pltpu.HBM), pl.BlockSpec(memory_space=pltpu.HBM)],
        out_specs=(pl.BlockSpec(memory_space=pltpu.HBM), pl.BlockSpec(memory_space=pltpu.VMEM),
                   pl.BlockSpec(memory_space=pltpu.VMEM)),
        scratch_shapes=[
            pltpu.VMEM((NP, WQ, PW), BF16),
            pltpu.VMEM((NP, K, PW), BF16),
            pltpu.VMEM((NP, K, PW), BF16),
            pltpu.VMEM((2, 8, K, PW), BF16),
            pltpu.VMEM((2, 8, K, PW), BF16),
            pltpu.VMEM((2, CHUNKS, 6, K, CW), BF16),
            pltpu.VMEM((2, CHUNKS, 6, K, CW), BF16),
            pltpu.VMEM((2, CHUNKS, 2, K, HALF), BF16),
            pltpu.VMEM((2, CHUNKS, 2, K, HALF), BF16),
            pltpu.VMEM((8, K, PW), F32),
            pltpu.VMEM((2, 16, ROWS, WQ), F32),
            pltpu.VMEM((2, 16, ROWS, WQ), F32),
            pltpu.VMEM((2, ROWS, WQ), F32),
            pltpu.VMEM((2, 16, ROWS, WQ), F32),
            pltpu.VMEM((4, K, WQ), F32),
            pltpu.VMEM((2, 16, K // 2, 128), F32),
            pltpu.VMEM((16, 8, 128), F32),
            pltpu.VMEM((K // 2, 128), F32),
            pltpu.VMEM((K // 2, 128), F32),
            pltpu.VMEM((8, K // 2, 128), F32),
            pltpu.VMEM((K, K), F32),
            dma((NP,)), dma((NP,)), dma,
            dma((2, 2, 16)), dma((2, 2, 16)),
            dma((2, 8)), dma((2, 8)),
            dma((2, CHUNKS, 8)), dma((2, CHUNKS, 8)),
            dma((2, CHUNKS, 8)), dma((2, CHUNKS, 8)),
            dma((2, CHUNKS, 8)), dma((2, CHUNKS, 8)),
            dma((2, 16)), dma((2, 16)),
            dma((16,)), dma((16,)),
            dma((8,)), dma((8,)),
        ],
        compiler_params=pltpu.CompilerParams(collective_id=0, has_side_effects=True, vmem_limit_bytes=56 * 1024 * 1024),
    )(differences, start_block)
    return pl.pallas_call(
        write_directions,
        out_shape=(jax.ShapeDtypeStruct((K, WF), F32), jax.ShapeDtypeStruct((1, K), F32)),
        in_specs=[pl.BlockSpec(memory_space=pl.ANY), pl.BlockSpec(memory_space=pltpu.VMEM),
                  pl.BlockSpec(memory_space=pltpu.VMEM)],
        out_specs=(pl.BlockSpec(memory_space=pltpu.HBM), pl.BlockSpec(memory_space=pltpu.VMEM)),
        scratch_shapes=[pltpu.VMEM((NP, K, PW), BF16), pltpu.VMEM((K, WF), F32), dma((GROUPS,)), dma((GROUPS,))],
    )(pulled, factor, scores)


def solution(mesh):
    in_specs = (P("samp", "feat"), P(None, "feat"))
    out_specs = (P(None, "feat"), P("feat", None))
    return jax.shard_map(
        on_device, mesh=mesh, in_specs=in_specs, out_specs=out_specs, check_vma=False
    )
```

```python
import math

import jax
import jax.numpy as jnp
from jax import lax
from jax.experimental import pallas as pl
from jax.experimental.pallas import tpu as pltpu
from jax.sharding import PartitionSpec as P

FEATURES = 131072
K = 64
NS = 576
WF = 8192
NP = 16
PW = WF // NP
CHUNKS = 2
CW = PW // CHUNKS
HALF = CW // 2
ROWS = K // 16
WQ = NS + K
LOAD = 4
MESH = pl.DeviceIdType.MESH
F32 = jnp.float32
BF16 = jnp.bfloat16


def dot_nn(a, b):
    return lax.dot_general(a, b, (((1,), (0,)), ((), ())), preferred_element_type=F32)


def dot_nt(a, b):
    return lax.dot_general(a, b, (((1,), (1,)), ((), ())), preferred_element_type=F32)


def dot_exact(a, b):
    return lax.dot_general(a, b, (((1,), (0,)), ((), ())), preferred_element_type=F32, precision=lax.Precision.HIGHEST)


def inverse_factor(gram):
    row = lax.broadcasted_iota(jnp.int32, (8, 2 * K), 0)
    col = lax.broadcasted_iota(jnp.int32, (8, 2 * K), 1)
    wide = jnp.concatenate([gram, jnp.zeros((K, K), F32)], axis=1)
    m = [wide[8 * g:8 * g + 8, :] + jnp.where(col == row + (K + 8 * g), 1.0, 0.0) for g in range(8)]
    out = []
    for b in range(8):
        cols = [[jnp.broadcast_to(m[g][:, 8 * b + k:8 * b + k + 1], (8, 2 * K)) for k in range(8)] for g in range(b, 8)]
        diag = jnp.zeros((8, 2 * K), F32)
        for k in range(8):
            d = cols[0][k][k:k + 1, :]
            r = 1.0 / d
            diag = jnp.where(row == k, d, diag)
            pivot_row = m[b][k:k + 1, :] * r
            factor = [jnp.where(row > k, cols[0][k], 0.0)] + [cols[i][k] for i in range(1, 8 - b)]
            for i in range(8 - b):
                m[b + i] = m[b + i] - factor[i] * pivot_row
            for kk in range(k + 1, 8):
                t = cols[0][k][kk:kk + 1, :] * r
                for i in range(8 - b):
                    cols[i][kk] = cols[i][kk] - factor[i] * t
        inv = lax.rsqrt(diag)
        inv = inv * (1.5 - 0.5 * ((diag * inv) * inv))
        out.append((m[b] * inv)[:, K:])
    return jnp.concatenate(out, axis=0)


def pack(square):
    return jnp.concatenate([square[0:K // 2], square[K // 2:]], axis=1)


def unpack(wide):
    return jnp.concatenate([wide[:, 0:K], wide[:, K:]], axis=0)


def ring_hops(d, n):
    return min(d, n - d)


PLANE = sorted([(dx, dy) for dx in range(4) for dy in range(4) if dx or dy],
               key=lambda o: -(ring_hops(o[0], 4) + ring_hops(o[1], 4)))
COLUMN = [4, 3, 5, 2, 6, 1, 7]


PAIRS = [4, 3, 5, 1, 7, 2, 6, 0]


def kernel(d_hbm, s_hbm, x2_out, factor_ref, score_ref,
           dv, sv, x2, psend, precv, msg_s, msg_r, half_s, half_r, acc,
           qs, qr, qo, qg, qf, gg, cs, cr, cg, g2,
           d_sem, s_sem, o_sem, ar_s, ar_r, pair_s, pair_r, rs_s, rs_r,
           ag_s, ag_r, sib_s, sib_r, g_s, g_r, c_s, c_r):
    samp = lax.axis_index("samp")
    feat = lax.axis_index("feat")
    z = samp // 2
    c = samp % 2
    x = feat // 4
    y = feat % 4
    sibling = (z * 2 + (1 - c), feat)

    def chip(d):
        return (((z + d) % 8) * 2 + c, feat)

    def across(dx, dy):
        return ((x + dx) % 4) * 4 + (y + dy) % 4

    def send(src, dst, ssem, rsem, dev):
        pltpu.make_async_remote_copy(src_ref=src, dst_ref=dst, send_sem=ssem, recv_sem=rsem,
                                     device_id=dev, device_id_type=MESH).start()

    def wait(ref, sem):
        pltpu.make_async_copy(ref, ref, sem).wait()

    for p in range(NP):
        pltpu.make_async_copy(s_hbm.at[:, p * PW:(p + 1) * PW], sv.at[p], s_sem).start()
    for p in range(NP):
        pltpu.make_async_copy(d_hbm.at[:, p * PW:(p + 1) * PW], dv.at[p, 0:NS, :], d_sem.at[p // LOAD]).start()

    barrier = pltpu.get_barrier_semaphore()
    for dx, dy in PLANE:
        pl.semaphore_signal(barrier, inc=1, device_id=(samp, across(dx, dy)), device_id_type=MESH)
    for d in COLUMN:
        pl.semaphore_signal(barrier, inc=1, device_id=chip(d), device_id_type=MESH)
    pl.semaphore_signal(barrier, inc=1, device_id=sibling, device_id_type=MESH)

    def reduce_scatter_q(it, value):
        for j in range(16):
            qs[it, j] = value[j * ROWS:(j + 1) * ROWS, :]
        for dx, dy in PLANE:
            there = across(dx, dy)
            send(qs.at[it, there], qr.at[it, dx * 4 + dy], ar_s.at[it, 0], ar_r.at[it, 0], (samp, there))

    def gather_q(it):
        total = qs[it, feat]
        wait(qr.at[it, 1:16], ar_r.at[it, 0])
        for r in range(1, 16):
            total = total + qr[it, r]
        qo[it] = total
        qg[it, 0] = total
        for dx, dy in PLANE:
            send(qo.at[it], qg.at[it, dx * 4 + dy], ar_s.at[it, 1], ar_r.at[it, 1], (samp, across(dx, dy)))
        wait(qs.at[it, 1:16], ar_s.at[it, 0])

    def join_q(it):
        wait(qg.at[it, 1:16], ar_r.at[it, 1])
        for j in range(16):
            slot = ((x - j // 4 + 4) % 4) * 4 + (y - j % 4 + 4) % 4
            qf[2 + it, j * ROWS:(j + 1) * ROWS, :] = qg[it, slot]
        return qf[2 + it, :, 0:NS]

    def exchange_gram(it, gram):
        gg[it, 0] = pack(gram)
        for dx, dy in PLANE:
            send(gg.at[it, 0], gg.at[it, dx * 4 + dy], g_s.at[it], g_r.at[it], (samp, across(dx, dy)))

    def join_gram(it):
        wait(gg.at[it, 1:16], g_r.at[it])
        total = gg[it, 0]
        for j in range(1, 16):
            total = total + gg[it, j]
        return unpack(total)

    q = jnp.zeros((K, NS), F32)
    wait(sv, s_sem)
    for p in range(NP):
        if p % LOAD == 0:
            wait(dv.at[p:p + LOAD, 0:NS, :], d_sem.at[p // LOAD])
        q = q + dot_nt(sv[p], dv[p, 0:NS, :])
    pl.semaphore_wait(barrier, 23)
    reduce_scatter_q(0, jnp.concatenate([q, jnp.zeros((K, K), F32)], axis=1))

    def energy_step(p, total):
        wide = dv[p, 0:NS, :].astype(F32)
        return total + jnp.sum(wide * wide, axis=0, keepdims=True)

    energy = lax.fori_loop(0, NP, energy_step, jnp.zeros((1, PW), F32))
    cs[K // 2:, :] = jnp.broadcast_to(jnp.sum(energy, axis=1, keepdims=True), (8, 128))
    gather_q(0)
    projected = join_q(0).astype(BF16)

    def pull_and_scatter(it, projected):
        def compute(d):
            there = (z + d) % 8
            k = PAIRS.index(d)
            psend[it, k] = dot_nn(projected, dv[(1 - c) * 8 + there, 0:NS, :]).astype(BF16)
            group = 0 if k < 3 else 1 if k < 5 else 2 if k < 7 else 3
            send(psend.at[it, k], precv.at[it, k], pair_s.at[it], pair_r.at[it, group], sibling)
            acc[d] = dot_nn(projected, dv[c * 8 + there, 0:NS, :])

        def join(group):
            first, last = ((0, 3), (3, 5), (5, 7), (7, 8))[group]
            wait(precv.at[it, first:last], pair_r.at[it, group])

        def both(d):
            return acc[d] + precv[it, PAIRS.index(d)].astype(F32)

        def post(slot, ch, value, dev):
            msg_s[it, ch, slot] = value.astype(BF16)
            send(msg_s.at[it, ch, slot], msg_r.at[it, ch, slot], rs_s.at[it, 0], rs_r.at[it, ch, slot], dev)

        def post_half(slot, ch, value, dev):
            half_s[it, ch, slot] = value.astype(BF16)
            send(half_s.at[it, ch, slot], half_r.at[it, ch, slot], rs_s.at[it, 1], rs_r.at[it, ch, 6 + slot], dev)

        def arrived(slot, ch):
            wait(msg_r.at[it, ch, slot] if slot < 6 else half_r.at[it, ch, slot - 6], rs_r.at[it, ch, slot])

        def cols(ch):
            return slice(ch * CW, (ch + 1) * CW)

        compute(4)
        compute(3)
        compute(5)
        compute(2)
        join(0)
        part4, part3, part5 = both(4), both(3), both(5)
        for ch in range(CHUNKS):
            part = part4[:, cols(ch)]
            post_half(0, ch, part[:, 0:HALF], chip(2))
            post_half(1, ch, part[:, HALF:], chip(6))
            post(0, ch, part3[:, cols(ch)], chip(1))
            post(1, ch, part5[:, cols(ch)], chip(7))
        compute(6)
        compute(1)
        compute(7)
        join(1)
        part1, part7 = both(1), both(7)
        for ch in range(CHUNKS):
            post(2, ch, part1[:, cols(ch)], chip(1))
            post(3, ch, part7[:, cols(ch)], chip(7))
        compute(0)
        join(2)
        acc[2] = both(2)
        acc[6] = both(6)
        for ch in range(CHUNKS):
            arrived(0, ch)
            arrived(6, ch)
            part = acc[2, :, cols(ch)] + msg_r[it, ch, 0].astype(F32)
            half = half_r[it, ch, 0].astype(F32)
            post(4, ch, jnp.concatenate([part[:, 0:HALF] + half, part[:, HALF:]], axis=1), chip(2))
            arrived(1, ch)
            arrived(7, ch)
            part = acc[6, :, cols(ch)] + msg_r[it, ch, 1].astype(F32)
            half = half_r[it, ch, 1].astype(F32)
            post(5, ch, jnp.concatenate([part[:, 0:HALF], part[:, HALF:] + half], axis=1), chip(6))
        join(3)
        acc[0] = both(0)
        for ch in range(CHUNKS):
            arrived(2, ch)
            arrived(3, ch)
            part = acc[0, :, cols(ch)] + msg_r[it, ch, 2].astype(F32) + msg_r[it, ch, 3].astype(F32)
            arrived(4, ch)
            arrived(5, ch)
            yield (part + msg_r[it, ch, 4].astype(F32) + msg_r[it, ch, 5].astype(F32)).astype(BF16)

    def gather(it, slot, pieces, use):
        here = c * 8
        there = (1 - c) * 8

        def pass_on(k, ch, d, dev, start=0, width=CW):
            ref = slot(here + (z + d) % 8, slice(ch * CW + start, ch * CW + start + width))
            send(ref, ref, ag_s.at[it, 1 if k in (4, 5) else 0], ag_r.at[it, ch, k], dev)

        def arrived(ch, k):
            wait(half_r.at[it, ch, 0] if k in (4, 5) else msg_r.at[it, ch, 0], ag_r.at[it, ch, k])

        def to_sibling(ch, d):
            ref = slot(here + (z + d) % 8, slice(ch * CW, (ch + 1) * CW))
            group = {0: 0, 6: 1, 2: 1, 7: 2, 1: 2, 5: 3, 3: 3, 4: 3}[d]
            send(ref, ref, sib_s.at[it], sib_r.at[it, ch, group], sibling)

        def use_own(ch, *ds):
            use([here + (z + d) % 8 for d in ds], slice(ch * CW, (ch + 1) * CW))

        def use_sibling(ch, *ds):
            group = {0: 0, 6: 1, 7: 2, 5: 3}[ds[0]]
            wait(msg_r.at[it, ch, 0:len(ds)], sib_r.at[it, ch, group])
            use([there + (z + d) % 8 for d in ds], slice(ch * CW, (ch + 1) * CW))

        for ch, piece in enumerate(pieces):
            slot(here + z, slice(ch * CW, (ch + 1) * CW))[...] = piece
            pass_on(0, ch, 0, chip(2))
            pass_on(1, ch, 0, chip(6))
            to_sibling(ch, 0)
        for ch in range(CHUNKS):
            pass_on(2, ch, 0, chip(1))
            pass_on(3, ch, 0, chip(7))
        use_own(0, 0)
        use_own(1, 0)
        use_sibling(0, 0)
        use_sibling(1, 0)
        for ch in range(CHUNKS):
            arrived(ch, 0)
            pass_on(4, ch, 6, chip(2), 0, HALF)
            pass_on(6, ch, 6, chip(1))
            to_sibling(ch, 6)
            arrived(ch, 1)
            pass_on(5, ch, 2, chip(6), HALF, HALF)
            pass_on(7, ch, 2, chip(7))
            to_sibling(ch, 2)
            use_own(ch, 6, 2)
        for ch in range(CHUNKS):
            arrived(ch, 2)
            to_sibling(ch, 7)
            arrived(ch, 3)
            to_sibling(ch, 1)
            use_own(ch, 7, 1)
            use_sibling(ch, 6, 2)
        use_sibling(0, 7, 1)
        use_sibling(1, 7, 1)
        for ch in range(CHUNKS):
            arrived(ch, 6)
            to_sibling(ch, 5)
            arrived(ch, 7)
            to_sibling(ch, 3)
            arrived(ch, 4)
            arrived(ch, 5)
            to_sibling(ch, 4)
            use_own(ch, 5, 3, 4)
        for ch in range(CHUNKS):
            use_sibling(ch, 5, 3, 4)

    qf[0] = jnp.zeros((K, WQ), F32)

    def use_first(ps, cols):
        qf[0] += sum(dot_nt(dv[p, NS:, cols], dv[p, :, cols]) for p in ps)

    gather(0, lambda p, cols: dv.at[p, NS:, cols], pull_and_scatter(0, projected), use_first)
    reduce_scatter_q(1, qf[0])
    exchange_gram(0, qf[0, :, NS:])
    gather_q(1)
    inv = inverse_factor(join_gram(0))
    projected = dot_exact(inv, join_q(1)).astype(BF16)

    qf[1] = jnp.zeros((K, WQ), F32)

    g2[...] = jnp.zeros((K, K), F32)

    def use_second(ps, cols):
        qf[1, :, 0:NS] += sum(dot_nt(x2[p, :, cols], dv[p, 0:NS, cols]) for p in ps)
        g2[...] += sum(dot_nt(x2[p, :, cols], x2[p, :, cols]) for p in ps)

    gather(1, lambda p, cols: x2.at[p, :, cols], pull_and_scatter(1, projected), use_second)
    exchange_gram(1, g2[...])
    for p in range(NP):
        pltpu.make_async_copy(x2.at[p], x2_out.at[:, p * PW:(p + 1) * PW], o_sem).start()

    along = qf[1, :, 0:NS]
    cs[0:K // 2, :] = pack(lax.dot_general(along, along, (((1,), (1,)), ((), ())), preferred_element_type=F32,
                                           precision=lax.Precision.HIGHEST))
    send(cs, cr, c_s.at[0], c_r.at[0], sibling)
    wait(cr, c_r.at[0])
    cg[0] = cs[...] + cr[...]
    for d in COLUMN:
        send(cg.at[0], cg.at[d], c_s.at[1], c_r.at[1], chip(d))

    wait(gg.at[0, 1:16], g_s.at[0])
    wait(qs.at[1, 1:16], ar_s.at[0, 1])
    wait(qs.at[1, 1:16], ar_s.at[1, 1])
    wait(cs, c_s.at[0])
    for it in range(2):
        wait(psend.at[it], pair_s.at[it])
        wait(msg_s.at[it], rs_s.at[it, 0])
        wait(half_s.at[it], rs_s.at[it, 1])
        wait(msg_s.at[it], ag_s.at[it, 0])
        wait(half_s.at[it], ag_s.at[it, 1])
        wait(psend.at[it], sib_s.at[it])

    inv = inverse_factor(join_gram(1))
    factor_ref[...] = inv * math.sqrt(FEATURES)
    wait(cg.at[1:8], c_r.at[1])
    total = cg[z]
    for j in range(1, 8):
        total = total + cg[(z - j + 8) % 8]
    spread = dot_exact(inv, unpack(total[0:K // 2])) * inv
    captured = lax.dot_general(jnp.ones((8, K), F32), spread, (((1,), (1,)), ((), ())),
                               preferred_element_type=F32, precision=lax.Precision.HIGHEST)
    score_ref[...] = FEATURES * captured[0:1, :] / (total[K // 2:K // 2 + 1, 0:K] + 1e-6)
    wait(gg.at[1, 1:16], g_s.at[1])
    wait(cg.at[1:8], c_s.at[1])
    wait(x2_out, o_sem)


def on_device(differences, start_block):
    dma = pltpu.SemaphoreType.DMA
    pulled, factor, scores = pl.pallas_call(
        kernel,
        out_shape=(jax.ShapeDtypeStruct((K, WF), BF16), jax.ShapeDtypeStruct((K, K), F32),
                   jax.ShapeDtypeStruct((1, K), F32)),
        in_specs=[pl.BlockSpec(memory_space=pltpu.HBM), pl.BlockSpec(memory_space=pltpu.HBM)],
        out_specs=(pl.BlockSpec(memory_space=pltpu.HBM), pl.BlockSpec(memory_space=pltpu.VMEM),
                   pl.BlockSpec(memory_space=pltpu.VMEM)),
        scratch_shapes=[
            pltpu.VMEM((NP, WQ, PW), BF16),
            pltpu.VMEM((NP, K, PW), BF16),
            pltpu.VMEM((NP, K, PW), BF16),
            pltpu.VMEM((2, 8, K, PW), BF16),
            pltpu.VMEM((2, 8, K, PW), BF16),
            pltpu.VMEM((2, CHUNKS, 6, K, CW), BF16),
            pltpu.VMEM((2, CHUNKS, 6, K, CW), BF16),
            pltpu.VMEM((2, CHUNKS, 2, K, HALF), BF16),
            pltpu.VMEM((2, CHUNKS, 2, K, HALF), BF16),
            pltpu.VMEM((8, K, PW), F32),
            pltpu.VMEM((2, 16, ROWS, WQ), F32),
            pltpu.VMEM((2, 16, ROWS, WQ), F32),
            pltpu.VMEM((2, ROWS, WQ), F32),
            pltpu.VMEM((2, 16, ROWS, WQ), F32),
            pltpu.VMEM((4, K, WQ), F32),
            pltpu.VMEM((2, 16, K // 2, 128), F32),
            pltpu.VMEM((K // 2 + 8, 128), F32),
            pltpu.VMEM((K // 2 + 8, 128), F32),
            pltpu.VMEM((8, K // 2 + 8, 128), F32),
            pltpu.VMEM((K, K), F32),
            dma((NP // LOAD,)), dma, dma,
            dma((2, 2)), dma((2, 2)),
            dma((2,)), dma((2, 4)),
            dma((2, 2)), dma((2, CHUNKS, 8)),
            dma((2, 2)), dma((2, CHUNKS, 8)),
            dma((2,)), dma((2, CHUNKS, 4)),
            dma((2,)), dma((2,)),
            dma((2,)), dma((2,)),
        ],
        compiler_params=pltpu.CompilerParams(collective_id=0, has_side_effects=True, vmem_limit_bytes=56 * 1024 * 1024),
    )(differences, start_block)
    directions = jnp.dot(factor, pulled.astype(F32), precision=lax.Precision.HIGH)
    return directions, scores


def solution(mesh):
    in_specs = (P("samp", "feat"), P(None, "feat"))
    out_specs = (P(None, "feat"), P("feat", None))
    return jax.shard_map(
        on_device, mesh=mesh, in_specs=in_specs, out_specs=out_specs, check_vma=False
    )
```

```python
import math

import jax
import jax.numpy as jnp
from jax import lax
from jax.experimental import pallas as pl
from jax.experimental.pallas import tpu as pltpu
from jax.sharding import PartitionSpec as P

FEATURES = 131072
K = 64
H = K // 2
NS = 576
WF = 8192
NP = 16
PW = WF // NP
CHUNKS = 2
CW = PW // CHUNKS
HALF = CW // 2
ROWS = K // 16
WQ = NS + K
LOAD = 4
MESH = pl.DeviceIdType.MESH
F32 = jnp.float32
BF16 = jnp.bfloat16


def dot_nn(a, b):
    return lax.dot_general(a, b, (((1,), (0,)), ((), ())), preferred_element_type=F32)


def dot_nt(a, b):
    return lax.dot_general(a, b, (((1,), (1,)), ((), ())), preferred_element_type=F32)


def dot_exact(a, b):
    return lax.dot_general(a, b, (((1,), (0,)), ((), ())), preferred_element_type=F32, precision=lax.Precision.HIGHEST)


def inverse_factor(gram):
    row = lax.broadcasted_iota(jnp.int32, (8, 2 * K), 0)
    col = lax.broadcasted_iota(jnp.int32, (8, 2 * K), 1)
    wide = jnp.concatenate([gram, jnp.zeros((K, K), F32)], axis=1)
    m = [wide[8 * g:8 * g + 8, :] + jnp.where(col == row + (K + 8 * g), 1.0, 0.0) for g in range(8)]
    out = []
    for b in range(8):
        cols = [[jnp.broadcast_to(m[g][:, 8 * b + k:8 * b + k + 1], (8, 2 * K)) for k in range(8)] for g in range(b, 8)]
        diag = jnp.zeros((8, 2 * K), F32)
        for k in range(8):
            d = cols[0][k][k:k + 1, :]
            r = 1.0 / d
            diag = jnp.where(row == k, d, diag)
            pivot_row = m[b][k:k + 1, :] * r
            factor = [jnp.where(row > k, cols[0][k], 0.0)] + [cols[i][k] for i in range(1, 8 - b)]
            for i in range(8 - b):
                m[b + i] = m[b + i] - factor[i] * pivot_row
            for kk in range(k + 1, 8):
                t = cols[0][k][kk:kk + 1, :] * r
                for i in range(8 - b):
                    cols[i][kk] = cols[i][kk] - factor[i] * t
        inv = lax.rsqrt(diag)
        inv = inv * (1.5 - 0.5 * ((diag * inv) * inv))
        out.append((m[b] * inv)[:, K:])
    return jnp.concatenate(out, axis=0)


def pack(square):
    return jnp.concatenate([square[0:K // 2], square[K // 2:]], axis=1)


def unpack(wide):
    return jnp.concatenate([wide[:, 0:K], wide[:, K:]], axis=0)


def ring_hops(d, n):
    return min(d, n - d)


PLANE = sorted([(dx, dy) for dx in range(4) for dy in range(4) if dx or dy],
               key=lambda o: -(ring_hops(o[0], 4) + ring_hops(o[1], 4)))
COLUMN = [4, 3, 5, 2, 6, 1, 7]


PAIRS = [4, 3, 5, 1, 7, 2, 6, 0]


def kernel(d_hbm, s_hbm, x2_out, factor_ref, score_ref,
           dv, sv, x2, psend, precv, msg_s, msg_r, half_s, half_r, acc,
           qs, qr, qo, qg, qf, gg, cs, cr, cg, g2, keep,
           d_sem, s_sem, o_sem, ar_s, ar_r, pair_s, pair_r, rs_s, rs_r,
           ag_s, ag_r, sib_s, sib_r, g_s, g_r, c_s, c_r):
    samp = lax.axis_index("samp")
    feat = lax.axis_index("feat")
    z = samp // 2
    c = samp % 2
    x = feat // 4
    y = feat % 4
    sibling = (z * 2 + (1 - c), feat)

    def chip(d):
        return (((z + d) % 8) * 2 + c, feat)

    def across(dx, dy):
        return ((x + dx) % 4) * 4 + (y + dy) % 4

    def send(src, dst, ssem, rsem, dev):
        pltpu.make_async_remote_copy(src_ref=src, dst_ref=dst, send_sem=ssem, recv_sem=rsem,
                                     device_id=dev, device_id_type=MESH).start()

    def wait(ref, sem):
        pltpu.make_async_copy(ref, ref, sem).wait()

    for p in range(NP):
        pltpu.make_async_copy(s_hbm.at[:, p * PW:(p + 1) * PW], sv.at[p], s_sem).start()
    for p in range(NP):
        pltpu.make_async_copy(d_hbm.at[:, p * PW:(p + 1) * PW], dv.at[p, 0:NS, :], d_sem.at[p // LOAD]).start()

    barrier = pltpu.get_barrier_semaphore()
    for dx, dy in PLANE:
        pl.semaphore_signal(barrier, inc=1, device_id=(samp, across(dx, dy)), device_id_type=MESH)
    for d in COLUMN:
        pl.semaphore_signal(barrier, inc=1, device_id=chip(d), device_id_type=MESH)
    pl.semaphore_signal(barrier, inc=1, device_id=sibling, device_id_type=MESH)

    def reduce_scatter_q(it, value):
        for j in range(16):
            qs[it, j] = value[j * ROWS:(j + 1) * ROWS, :]
        for dx, dy in PLANE:
            there = across(dx, dy)
            send(qs.at[it, there], qr.at[it, dx * 4 + dy], ar_s.at[it, 0], ar_r.at[it, 0], (samp, there))

    def gather_q(it):
        total = qs[it, feat]
        wait(qr.at[it, 1:16], ar_r.at[it, 0])
        for r in range(1, 16):
            total = total + qr[it, r]
        qo[it] = total
        qg[it, 0] = total
        for dx, dy in PLANE:
            send(qo.at[it], qg.at[it, dx * 4 + dy], ar_s.at[it, 1], ar_r.at[it, 1], (samp, across(dx, dy)))
        wait(qs.at[it, 1:16], ar_s.at[it, 0])

    def join_q(it):
        wait(qg.at[it, 1:16], ar_r.at[it, 1])
        for j in range(16):
            slot = ((x - j // 4 + 4) % 4) * 4 + (y - j % 4 + 4) % 4
            qf[2 + it, j * ROWS:(j + 1) * ROWS, :] = qg[it, slot]
        return qf[2 + it, :, 0:NS]

    def exchange_gram(it, gram):
        gg[it, 0] = pack(gram)
        for dx, dy in PLANE:
            send(gg.at[it, 0], gg.at[it, dx * 4 + dy], g_s.at[it], g_r.at[it], (samp, across(dx, dy)))

    def join_gram(it):
        wait(gg.at[it, 1:16], g_r.at[it])
        total = gg[it, 0]
        for j in range(1, 16):
            total = total + gg[it, j]
        return unpack(total)

    q = jnp.zeros((K, NS), F32)
    wait(sv, s_sem)
    for p in range(NP):
        if p % LOAD == 0:
            wait(dv.at[p:p + LOAD, 0:NS, :], d_sem.at[p // LOAD])
        q = q + dot_nt(sv[p], dv[p, 0:NS, :])
    pl.semaphore_wait(barrier, 23)
    reduce_scatter_q(0, jnp.concatenate([q, jnp.zeros((K, K), F32)], axis=1))

    def energy_step(p, total):
        wide = dv[p, 0:NS, :].astype(F32)
        return total + jnp.sum(wide * wide, axis=0, keepdims=True)

    energy = lax.fori_loop(0, NP, energy_step, jnp.zeros((1, PW), F32))
    keep[...] = jnp.broadcast_to(jnp.sum(energy, axis=1, keepdims=True), (8, 128))
    gather_q(0)
    projected = join_q(0).astype(BF16)

    def pull_and_scatter(it, projected):
        def compute(d):
            there = (z + d) % 8
            k = PAIRS.index(d)
            psend[it, k] = dot_nn(projected, dv[(1 - c) * 8 + there, 0:NS, :]).astype(BF16)
            group = 0 if k < 3 else 1 if k < 5 else 2 if k < 7 else 3
            send(psend.at[it, k], precv.at[it, k], pair_s.at[it], pair_r.at[it, group], sibling)
            acc[d] = dot_nn(projected, dv[c * 8 + there, 0:NS, :])

        def join(group):
            first, last = ((0, 3), (3, 5), (5, 7), (7, 8))[group]
            wait(precv.at[it, first:last], pair_r.at[it, group])

        def both(d):
            return acc[d] + precv[it, PAIRS.index(d)].astype(F32)

        def post(slot, ch, value, dev):
            msg_s[it, ch, slot] = value.astype(BF16)
            send(msg_s.at[it, ch, slot], msg_r.at[it, ch, slot], rs_s.at[it, 0], rs_r.at[it, ch, slot], dev)

        def post_half(slot, ch, value, dev):
            half_s[it, ch, slot] = value.astype(BF16)
            send(half_s.at[it, ch, slot], half_r.at[it, ch, slot], rs_s.at[it, 1], rs_r.at[it, ch, 6 + slot], dev)

        def arrived(slot, ch):
            wait(msg_r.at[it, ch, slot] if slot < 6 else half_r.at[it, ch, slot - 6], rs_r.at[it, ch, slot])

        def cols(ch):
            return slice(ch * CW, (ch + 1) * CW)

        compute(4)
        compute(3)
        compute(5)
        compute(2)
        join(0)
        part4, part3, part5 = both(4), both(3), both(5)
        for ch in range(CHUNKS):
            part = part4[:, cols(ch)]
            post_half(0, ch, part[:, 0:HALF], chip(2))
            post_half(1, ch, part[:, HALF:], chip(6))
            post(0, ch, part3[:, cols(ch)], chip(1))
            post(1, ch, part5[:, cols(ch)], chip(7))
        compute(6)
        compute(1)
        compute(7)
        join(1)
        part1, part7 = both(1), both(7)
        for ch in range(CHUNKS):
            post(2, ch, part1[:, cols(ch)], chip(1))
            post(3, ch, part7[:, cols(ch)], chip(7))
        compute(0)
        join(2)
        acc[2] = both(2)
        acc[6] = both(6)
        for ch in range(CHUNKS):
            arrived(0, ch)
            arrived(6, ch)
            part = acc[2, :, cols(ch)] + msg_r[it, ch, 0].astype(F32)
            half = half_r[it, ch, 0].astype(F32)
            post(4, ch, jnp.concatenate([part[:, 0:HALF] + half, part[:, HALF:]], axis=1), chip(2))
            arrived(1, ch)
            arrived(7, ch)
            part = acc[6, :, cols(ch)] + msg_r[it, ch, 1].astype(F32)
            half = half_r[it, ch, 1].astype(F32)
            post(5, ch, jnp.concatenate([part[:, 0:HALF], part[:, HALF:] + half], axis=1), chip(6))
        join(3)
        acc[0] = both(0)
        for ch in range(CHUNKS):
            arrived(2, ch)
            arrived(3, ch)
            part = acc[0, :, cols(ch)] + msg_r[it, ch, 2].astype(F32) + msg_r[it, ch, 3].astype(F32)
            arrived(4, ch)
            arrived(5, ch)
            yield (part + msg_r[it, ch, 4].astype(F32) + msg_r[it, ch, 5].astype(F32)).astype(BF16)

    def gather(it, slot, pieces, use):
        here = c * 8
        there = (1 - c) * 8

        def pass_on(k, ch, d, dev, start=0, width=CW):
            ref = slot(here + (z + d) % 8, slice(ch * CW + start, ch * CW + start + width))
            send(ref, ref, ag_s.at[it, 1 if k in (4, 5) else 0], ag_r.at[it, ch, k], dev)

        def arrived(ch, k):
            wait(half_r.at[it, ch, 0] if k in (4, 5) else msg_r.at[it, ch, 0], ag_r.at[it, ch, k])

        def to_sibling(ch, d):
            ref = slot(here + (z + d) % 8, slice(ch * CW, (ch + 1) * CW))
            group = {0: 0, 6: 1, 2: 1, 7: 2, 1: 2, 5: 3, 3: 3, 4: 3}[d]
            send(ref, ref, sib_s.at[it], sib_r.at[it, ch, group], sibling)

        def use_own(ch, *ds):
            use([here + (z + d) % 8 for d in ds], slice(ch * CW, (ch + 1) * CW))

        def use_sibling(ch, *ds):
            group = {0: 0, 6: 1, 7: 2, 5: 3}[ds[0]]
            wait(msg_r.at[it, ch, 0:len(ds)], sib_r.at[it, ch, group])
            use([there + (z + d) % 8 for d in ds], slice(ch * CW, (ch + 1) * CW))

        for ch, piece in enumerate(pieces):
            slot(here + z, slice(ch * CW, (ch + 1) * CW))[...] = piece
            pass_on(0, ch, 0, chip(2))
            pass_on(1, ch, 0, chip(6))
            to_sibling(ch, 0)
        for ch in range(CHUNKS):
            pass_on(2, ch, 0, chip(1))
            pass_on(3, ch, 0, chip(7))
        use_own(0, 0)
        use_own(1, 0)
        use_sibling(0, 0)
        use_sibling(1, 0)
        for ch in range(CHUNKS):
            arrived(ch, 0)
            pass_on(4, ch, 6, chip(2), 0, HALF)
            pass_on(6, ch, 6, chip(1))
            to_sibling(ch, 6)
            arrived(ch, 1)
            pass_on(5, ch, 2, chip(6), HALF, HALF)
            pass_on(7, ch, 2, chip(7))
            to_sibling(ch, 2)
            use_own(ch, 6, 2)
        for ch in range(CHUNKS):
            arrived(ch, 2)
            to_sibling(ch, 7)
            arrived(ch, 3)
            to_sibling(ch, 1)
            use_own(ch, 7, 1)
            use_sibling(ch, 6, 2)
        use_sibling(0, 7, 1)
        use_sibling(1, 7, 1)
        for ch in range(CHUNKS):
            arrived(ch, 6)
            to_sibling(ch, 5)
            arrived(ch, 7)
            to_sibling(ch, 3)
            arrived(ch, 4)
            arrived(ch, 5)
            to_sibling(ch, 4)
            use_own(ch, 5, 3, 4)
        for ch in range(CHUNKS):
            use_sibling(ch, 5, 3, 4)

    qf[0] = jnp.zeros((K, WQ), F32)

    def use_first(ps, cols):
        qf[0] += sum(dot_nt(dv[p, NS:, cols], dv[p, :, cols]) for p in ps)

    gather(0, lambda p, cols: dv.at[p, NS:, cols], pull_and_scatter(0, projected), use_first)
    reduce_scatter_q(1, qf[0])
    exchange_gram(0, qf[0, :, NS:])
    gather_q(1)
    inv = inverse_factor(join_gram(0))
    projected = dot_exact(inv, join_q(1)).astype(BF16)

    qf[1] = jnp.zeros((K, WQ), F32)

    g2[...] = jnp.zeros((K, K), F32)

    def use_second(ps, cols):
        qf[1, :, 0:NS] += sum(dot_nt(x2[p, :, cols], dv[p, 0:NS, cols]) for p in ps)
        g2[...] += sum(dot_nt(x2[p, :, cols], x2[p, :, cols]) for p in ps)

    gather(1, lambda p, cols: x2.at[p, :, cols], pull_and_scatter(1, projected), use_second)
    exchange_gram(1, g2[...])
    for p in range(NP):
        pltpu.make_async_copy(x2.at[p], x2_out.at[:, p * PW:(p + 1) * PW], o_sem).start()

    along = qf[1, :, 0:NS]
    high = along.astype(BF16)
    rest = along - high.astype(F32)
    middle = rest.astype(BF16)
    low = (rest - middle.astype(F32)).astype(BF16)
    parts = jnp.concatenate([high, middle, low], axis=0)
    nine = dot_nt(parts, parts)
    rows = nine[0:K] + nine[K:2 * K] + nine[2 * K:]
    square = rows[:, 0:K] + rows[:, K:2 * K] + rows[:, 2 * K:]
    cs[...] = jnp.concatenate([square[0:H, :], square[H:, H:], jnp.broadcast_to(keep[0:1, 0:H], (H, H))], axis=1)
    send(cs, cr, c_s.at[0], c_r.at[0], sibling)
    wait(cr, c_r.at[0])
    cg[0] = cs[...] + cr[...]
    for d in COLUMN:
        send(cg.at[0], cg.at[d], c_s.at[1], c_r.at[1], chip(d))

    wait(gg.at[0, 1:16], g_s.at[0])
    wait(qs.at[1, 1:16], ar_s.at[0, 1])
    wait(qs.at[1, 1:16], ar_s.at[1, 1])
    wait(cs, c_s.at[0])
    for it in range(2):
        wait(psend.at[it], pair_s.at[it])
        wait(msg_s.at[it], rs_s.at[it, 0])
        wait(half_s.at[it], rs_s.at[it, 1])
        wait(msg_s.at[it], ag_s.at[it, 0])
        wait(half_s.at[it], ag_s.at[it, 1])
        wait(psend.at[it], sib_s.at[it])

    inv = inverse_factor(join_gram(1))
    factor_ref[...] = inv * math.sqrt(FEATURES)
    wait(cg.at[1:8], c_r.at[1])
    total = cg[z]
    for j in range(1, 8):
        total = total + cg[(z - j + 8) % 8]
    once = lax.broadcasted_iota(jnp.int32, (H, K), 1) < H
    form = jnp.concatenate([jnp.where(once, total[:, 0:K], 2.0 * total[:, 0:K]),
                            jnp.concatenate([jnp.zeros((H, H), F32), total[:, K:K + H]], axis=1)], axis=0)
    spread = dot_exact(inv, form) * inv
    captured = lax.dot_general(jnp.ones((8, K), F32), spread, (((1,), (1,)), ((), ())),
                               preferred_element_type=F32, precision=lax.Precision.HIGHEST)
    score_ref[...] = FEATURES * captured[0:1, :] / (total[0:1, K + H:K + H + 1] + 1e-6)
    wait(gg.at[1, 1:16], g_s.at[1])
    wait(cg.at[1:8], c_s.at[1])
    wait(x2_out, o_sem)


def on_device(differences, start_block):
    dma = pltpu.SemaphoreType.DMA
    pulled, factor, scores = pl.pallas_call(
        kernel,
        out_shape=(jax.ShapeDtypeStruct((K, WF), BF16), jax.ShapeDtypeStruct((K, K), F32),
                   jax.ShapeDtypeStruct((1, K), F32)),
        in_specs=[pl.BlockSpec(memory_space=pltpu.HBM), pl.BlockSpec(memory_space=pltpu.HBM)],
        out_specs=(pl.BlockSpec(memory_space=pltpu.HBM), pl.BlockSpec(memory_space=pltpu.VMEM),
                   pl.BlockSpec(memory_space=pltpu.VMEM)),
        scratch_shapes=[
            pltpu.VMEM((NP, WQ, PW), BF16),
            pltpu.VMEM((NP, K, PW), BF16),
            pltpu.VMEM((NP, K, PW), BF16),
            pltpu.VMEM((2, 8, K, PW), BF16),
            pltpu.VMEM((2, 8, K, PW), BF16),
            pltpu.VMEM((2, CHUNKS, 6, K, CW), BF16),
            pltpu.VMEM((2, CHUNKS, 6, K, CW), BF16),
            pltpu.VMEM((2, CHUNKS, 2, K, HALF), BF16),
            pltpu.VMEM((2, CHUNKS, 2, K, HALF), BF16),
            pltpu.VMEM((8, K, PW), F32),
            pltpu.VMEM((2, 16, ROWS, WQ), F32),
            pltpu.VMEM((2, 16, ROWS, WQ), F32),
            pltpu.VMEM((2, ROWS, WQ), F32),
            pltpu.VMEM((2, 16, ROWS, WQ), F32),
            pltpu.VMEM((4, K, WQ), F32),
            pltpu.VMEM((2, 16, K // 2, 128), F32),
            pltpu.VMEM((H, 128), F32),
            pltpu.VMEM((H, 128), F32),
            pltpu.VMEM((8, H, 128), F32),
            pltpu.VMEM((K, K), F32),
            pltpu.VMEM((8, 128), F32),
            dma((NP // LOAD,)), dma, dma,
            dma((2, 2)), dma((2, 2)),
            dma((2,)), dma((2, 4)),
            dma((2, 2)), dma((2, CHUNKS, 8)),
            dma((2, 2)), dma((2, CHUNKS, 8)),
            dma((2,)), dma((2, CHUNKS, 4)),
            dma((2,)), dma((2,)),
            dma((2,)), dma((2,)),
        ],
        compiler_params=pltpu.CompilerParams(collective_id=0, has_side_effects=True, vmem_limit_bytes=52 * 1024 * 1024),
    )(differences, start_block)
    directions = jnp.dot(factor, pulled.astype(F32), precision=lax.Precision.HIGH)
    return directions, scores


def solution(mesh):
    in_specs = (P("samp", "feat"), P(None, "feat"))
    out_specs = (P(None, "feat"), P("feat", None))
    return jax.shard_map(
        on_device, mesh=mesh, in_specs=in_specs, out_specs=out_specs, check_vma=False
    )
```

```python
import math

import jax
import jax.numpy as jnp
from jax import lax
from jax.experimental import pallas as pl
from jax.experimental.pallas import tpu as pltpu
from jax.sharding import PartitionSpec as P

FEATURES = 131072
K = 64
H = K // 2
NS = 576
WF = 8192
NP = 16
PW = WF // NP
CHUNKS = 2
CW = PW // CHUNKS
HALF = CW // 2
ROWS = K // 16
WQ = NS + K
LOAD = 4
MESH = pl.DeviceIdType.MESH
F32 = jnp.float32
BF16 = jnp.bfloat16


def dot_nn(a, b):
    return lax.dot_general(a, b, (((1,), (0,)), ((), ())), preferred_element_type=F32)


def dot_nt(a, b):
    return lax.dot_general(a, b, (((1,), (1,)), ((), ())), preferred_element_type=F32)


def dot_exact(a, b):
    return lax.dot_general(a, b, (((1,), (0,)), ((), ())), preferred_element_type=F32, precision=lax.Precision.HIGHEST)


def inverse_factor(gram):
    row = lax.broadcasted_iota(jnp.int32, (8, 2 * K), 0)
    col = lax.broadcasted_iota(jnp.int32, (8, 2 * K), 1)
    wide = jnp.concatenate([gram, jnp.zeros((K, K), F32)], axis=1)
    m = [wide[8 * g:8 * g + 8, :] + jnp.where(col == row + (K + 8 * g), 1.0, 0.0) for g in range(8)]
    out = []
    for b in range(8):
        cols = [[jnp.broadcast_to(m[g][:, 8 * b + k:8 * b + k + 1], (8, 2 * K)) for k in range(8)] for g in range(b, 8)]
        diag = jnp.zeros((8, 2 * K), F32)
        for k in range(8):
            d = cols[0][k][k:k + 1, :]
            r = 1.0 / d
            diag = jnp.where(row == k, d, diag)
            pivot_row = m[b][k:k + 1, :] * r
            factor = [jnp.where(row > k, cols[0][k], 0.0)] + [cols[i][k] for i in range(1, 8 - b)]
            for i in range(8 - b):
                m[b + i] = m[b + i] - factor[i] * pivot_row
            for kk in range(k + 1, 8):
                t = cols[0][k][kk:kk + 1, :] * r
                for i in range(8 - b):
                    cols[i][kk] = cols[i][kk] - factor[i] * t
        inv = lax.rsqrt(diag)
        inv = inv * (1.5 - 0.5 * ((diag * inv) * inv))
        out.append((m[b] * inv)[:, K:])
    return jnp.concatenate(out, axis=0)


def pack(square):
    return jnp.concatenate([square[0:K // 2], square[K // 2:]], axis=1)


def unpack(wide):
    return jnp.concatenate([wide[:, 0:K], wide[:, K:]], axis=0)


def ring_hops(d, n):
    return min(d, n - d)


PLANE = sorted([(dx, dy) for dx in range(4) for dy in range(4) if dx or dy],
               key=lambda o: -(ring_hops(o[0], 4) + ring_hops(o[1], 4)))
COLUMN = [4, 3, 5, 2, 6, 1, 7]


PAIRS = [4, 3, 5, 1, 7, 2, 6, 0]


def kernel(d_hbm, s_hbm, x2_out, factor_ref, score_ref,
           dv, sv, x2, psend, precv, msg_s, msg_r, half_s, half_r, acc,
           qs, qr, qo, qg, qf, gg, cs, cr, cg, g2, keep,
           d_sem, s_sem, o_sem, ar_s, ar_r, pair_s, pair_r, rs_s, rs_r,
           ag_s, ag_r, sib_s, sib_r, g_s, g_r, c_s, c_r):
    samp = lax.axis_index("samp")
    feat = lax.axis_index("feat")
    z = samp // 2
    c = samp % 2
    x = feat // 4
    y = feat % 4
    sibling = (z * 2 + (1 - c), feat)

    def chip(d):
        return (((z + d) % 8) * 2 + c, feat)

    def across(dx, dy):
        return ((x + dx) % 4) * 4 + (y + dy) % 4

    def send(src, dst, ssem, rsem, dev):
        pltpu.make_async_remote_copy(src_ref=src, dst_ref=dst, send_sem=ssem, recv_sem=rsem,
                                     device_id=dev, device_id_type=MESH).start()

    def wait(ref, sem):
        pltpu.make_async_copy(ref, ref, sem).wait()

    for p in range(NP):
        pltpu.make_async_copy(s_hbm.at[:, p * PW:(p + 1) * PW], sv.at[p], s_sem).start()
    for p in range(NP):
        pltpu.make_async_copy(d_hbm.at[:, p * PW:(p + 1) * PW], dv.at[p, 0:NS, :], d_sem.at[p // LOAD]).start()

    barrier = pltpu.get_barrier_semaphore()
    for dx, dy in PLANE:
        pl.semaphore_signal(barrier, inc=1, device_id=(samp, across(dx, dy)), device_id_type=MESH)
    for d in COLUMN:
        pl.semaphore_signal(barrier, inc=1, device_id=chip(d), device_id_type=MESH)
    pl.semaphore_signal(barrier, inc=1, device_id=sibling, device_id_type=MESH)

    def reduce_scatter_q(it, value):
        for j in range(16):
            qs[it, j] = value[j * ROWS:(j + 1) * ROWS, :]
        for dx, dy in PLANE:
            there = across(dx, dy)
            send(qs.at[it, there], qr.at[it, dx * 4 + dy], ar_s.at[it, 0], ar_r.at[it, 0], (samp, there))

    def gather_q(it):
        total = qs[it, feat]
        wait(qr.at[it, 1:16], ar_r.at[it, 0])
        for r in range(1, 16):
            total = total + qr[it, r]
        qo[it] = total
        qg[it, 0] = total
        for dx, dy in PLANE:
            send(qo.at[it], qg.at[it, dx * 4 + dy], ar_s.at[it, 1], ar_r.at[it, 1], (samp, across(dx, dy)))
        wait(qs.at[it, 1:16], ar_s.at[it, 0])

    def join_q(it):
        wait(qg.at[it, 1:16], ar_r.at[it, 1])
        for j in range(16):
            slot = ((x - j // 4 + 4) % 4) * 4 + (y - j % 4 + 4) % 4
            qf[2 + it, j * ROWS:(j + 1) * ROWS, :] = qg[it, slot]
        return qf[2 + it, :, 0:NS]

    def exchange_gram(it, gram):
        gg[it, 0] = pack(gram)
        for dx, dy in PLANE:
            send(gg.at[it, 0], gg.at[it, dx * 4 + dy], g_s.at[it], g_r.at[it], (samp, across(dx, dy)))

    def join_gram(it):
        wait(gg.at[it, 1:16], g_r.at[it])
        total = gg[it, 0]
        for j in range(1, 16):
            total = total + gg[it, j]
        return unpack(total)

    q = jnp.zeros((K, NS), F32)
    wait(sv, s_sem)
    for p in range(NP):
        if p % LOAD == 0:
            wait(dv.at[p:p + LOAD, 0:NS, :], d_sem.at[p // LOAD])
        q = q + dot_nt(sv[p], dv[p, 0:NS, :])
    pl.semaphore_wait(barrier, 23)
    reduce_scatter_q(0, jnp.concatenate([q, jnp.zeros((K, K), F32)], axis=1))

    def energy_step(p, total):
        wide = dv[p, 0:NS, :].astype(F32)
        return total + jnp.sum(wide * wide, axis=0, keepdims=True)

    energy = lax.fori_loop(0, NP, energy_step, jnp.zeros((1, PW), F32))
    keep[...] = jnp.broadcast_to(jnp.sum(energy, axis=1, keepdims=True), (8, 128))
    gather_q(0)
    projected = join_q(0).astype(BF16)

    def pull_and_scatter(it, projected):
        def theirs(*ds):
            for d in ds:
                k = PAIRS.index(d)
                psend[it, k] = dot_nn(projected, dv[(1 - c) * 8 + (z + d) % 8, 0:NS, :]).astype(BF16)
                send(psend.at[it, k], precv.at[it, k], pair_s.at[it], pair_r.at[it, (k + 1) // 2], sibling)

        def ours(*ds):
            for d in ds:
                acc[d] = dot_nn(projected, dv[c * 8 + (z + d) % 8, 0:NS, :])

        def join(group):
            first, last = ((0, 1), (1, 3), (3, 5), (5, 7), (7, 8))[group]
            wait(precv.at[it, first:last], pair_r.at[it, group])

        def both(d):
            return acc[d] + precv[it, PAIRS.index(d)].astype(F32)

        def post(slot, ch, value, dev):
            msg_s[it, ch, slot] = value.astype(BF16)
            send(msg_s.at[it, ch, slot], msg_r.at[it, ch, slot], rs_s.at[it, 0], rs_r.at[it, ch, slot], dev)

        def post_half(slot, ch, value, dev):
            half_s[it, ch, slot] = value.astype(BF16)
            send(half_s.at[it, ch, slot], half_r.at[it, ch, slot], rs_s.at[it, 1], rs_r.at[it, ch, 6 + slot], dev)

        def arrived(slot, ch):
            wait(msg_r.at[it, ch, slot] if slot < 6 else half_r.at[it, ch, slot - 6], rs_r.at[it, ch, slot])

        def cols(ch):
            return slice(ch * CW, (ch + 1) * CW)

        theirs(4, 3, 5)
        ours(4, 3, 5)
        theirs(1, 7)
        join(0)
        part4 = both(4)
        for ch in range(CHUNKS):
            part = part4[:, cols(ch)]
            post_half(0, ch, part[:, 0:HALF], chip(2))
            post_half(1, ch, part[:, HALF:], chip(6))
        join(1)
        part3, part5 = both(3), both(5)
        for ch in range(CHUNKS):
            post(0, ch, part3[:, cols(ch)], chip(1))
            post(1, ch, part5[:, cols(ch)], chip(7))
        ours(1, 7)
        theirs(2, 6, 0)
        join(2)
        part1, part7 = both(1), both(7)
        for ch in range(CHUNKS):
            post(2, ch, part1[:, cols(ch)], chip(1))
            post(3, ch, part7[:, cols(ch)], chip(7))
        ours(2, 6, 0)
        join(3)
        acc[2] = both(2)
        acc[6] = both(6)
        for ch in range(CHUNKS):
            arrived(0, ch)
            arrived(6, ch)
            part = acc[2, :, cols(ch)] + msg_r[it, ch, 0].astype(F32)
            half = half_r[it, ch, 0].astype(F32)
            post(4, ch, jnp.concatenate([part[:, 0:HALF] + half, part[:, HALF:]], axis=1), chip(2))
            arrived(1, ch)
            arrived(7, ch)
            part = acc[6, :, cols(ch)] + msg_r[it, ch, 1].astype(F32)
            half = half_r[it, ch, 1].astype(F32)
            post(5, ch, jnp.concatenate([part[:, 0:HALF], part[:, HALF:] + half], axis=1), chip(6))
        join(4)
        acc[0] = both(0)
        for ch in range(CHUNKS):
            arrived(2, ch)
            arrived(3, ch)
            part = acc[0, :, cols(ch)] + msg_r[it, ch, 2].astype(F32) + msg_r[it, ch, 3].astype(F32)
            arrived(4, ch)
            arrived(5, ch)
            yield (part + msg_r[it, ch, 4].astype(F32) + msg_r[it, ch, 5].astype(F32)).astype(BF16)

    def gather(it, slot, pieces, use):
        here = c * 8
        there = (1 - c) * 8

        def pass_on(k, ch, d, dev, start=0, width=CW):
            ref = slot(here + (z + d) % 8, slice(ch * CW + start, ch * CW + start + width))
            send(ref, ref, ag_s.at[it, 1 if k in (4, 5) else 0], ag_r.at[it, ch, k], dev)

        def arrived(ch, k):
            wait(half_r.at[it, ch, 0] if k in (4, 5) else msg_r.at[it, ch, 0], ag_r.at[it, ch, k])

        def to_sibling(ch, d):
            ref = slot(here + (z + d) % 8, slice(ch * CW, (ch + 1) * CW))
            group = {0: 0, 6: 1, 2: 1, 7: 2, 1: 2, 5: 3, 3: 3, 4: 3}[d]
            send(ref, ref, sib_s.at[it], sib_r.at[it, ch, group], sibling)

        def use_own(ch, *ds):
            use([here + (z + d) % 8 for d in ds], slice(ch * CW, (ch + 1) * CW))

        def use_sibling(ch, *ds):
            group = {0: 0, 6: 1, 7: 2, 5: 3}[ds[0]]
            wait(msg_r.at[it, ch, 0:len(ds)], sib_r.at[it, ch, group])
            use([there + (z + d) % 8 for d in ds], slice(ch * CW, (ch + 1) * CW))

        for ch, piece in enumerate(pieces):
            slot(here + z, slice(ch * CW, (ch + 1) * CW))[...] = piece
            pass_on(0, ch, 0, chip(2))
            pass_on(1, ch, 0, chip(6))
            to_sibling(ch, 0)
        for ch in range(CHUNKS):
            pass_on(2, ch, 0, chip(1))
            pass_on(3, ch, 0, chip(7))
        use_own(0, 0)
        use_own(1, 0)
        use_sibling(0, 0)
        use_sibling(1, 0)
        for ch in range(CHUNKS):
            arrived(ch, 0)
            pass_on(4, ch, 6, chip(2), 0, HALF)
            pass_on(6, ch, 6, chip(1))
            to_sibling(ch, 6)
            arrived(ch, 1)
            pass_on(5, ch, 2, chip(6), HALF, HALF)
            pass_on(7, ch, 2, chip(7))
            to_sibling(ch, 2)
            use_own(ch, 6, 2)
        for ch in range(CHUNKS):
            arrived(ch, 2)
            to_sibling(ch, 7)
            arrived(ch, 3)
            to_sibling(ch, 1)
            use_own(ch, 7, 1)
            use_sibling(ch, 6, 2)
        use_sibling(0, 7, 1)
        use_sibling(1, 7, 1)
        for ch in range(CHUNKS):
            arrived(ch, 6)
            to_sibling(ch, 5)
            arrived(ch, 7)
            to_sibling(ch, 3)
            arrived(ch, 4)
            arrived(ch, 5)
            to_sibling(ch, 4)
            use_own(ch, 5, 3, 4)
        for ch in range(CHUNKS):
            use_sibling(ch, 5, 3, 4)

    qf[0] = jnp.zeros((K, WQ), F32)

    def use_first(ps, cols):
        qf[0] += sum(dot_nt(dv[p, NS:, cols], dv[p, :, cols]) for p in ps)

    gather(0, lambda p, cols: dv.at[p, NS:, cols], pull_and_scatter(0, projected), use_first)
    reduce_scatter_q(1, qf[0])
    exchange_gram(0, qf[0, :, NS:])
    gather_q(1)
    inv = inverse_factor(join_gram(0))
    projected = dot_exact(inv, join_q(1)).astype(BF16)

    qf[1] = jnp.zeros((K, WQ), F32)

    g2[...] = jnp.zeros((K, K), F32)

    def use_second(ps, cols):
        qf[1, :, 0:NS] += sum(dot_nt(x2[p, :, cols], dv[p, 0:NS, cols]) for p in ps)
        g2[...] += sum(dot_nt(x2[p, :, cols], x2[p, :, cols]) for p in ps)

    gather(1, lambda p, cols: x2.at[p, :, cols], pull_and_scatter(1, projected), use_second)
    exchange_gram(1, g2[...])
    for p in range(NP):
        pltpu.make_async_copy(x2.at[p], x2_out.at[:, p * PW:(p + 1) * PW], o_sem).start()

    along = qf[1, :, 0:NS]
    high = along.astype(BF16)
    rest = along - high.astype(F32)
    middle = rest.astype(BF16)
    low = (rest - middle.astype(F32)).astype(BF16)
    parts = jnp.concatenate([high, middle, low], axis=0)
    nine = dot_nt(parts, parts)
    rows = nine[0:K] + nine[K:2 * K] + nine[2 * K:]
    square = rows[:, 0:K] + rows[:, K:2 * K] + rows[:, 2 * K:]
    cs[...] = jnp.concatenate([square[0:H, :], square[H:, H:], jnp.broadcast_to(keep[0:1, 0:H], (H, H))], axis=1)
    send(cs, cr, c_s.at[0], c_r.at[0], sibling)
    wait(cr, c_r.at[0])
    cg[0] = cs[...] + cr[...]
    for d in COLUMN:
        send(cg.at[0], cg.at[d], c_s.at[1], c_r.at[1], chip(d))

    wait(gg.at[0, 1:16], g_s.at[0])
    wait(qs.at[1, 1:16], ar_s.at[0, 1])
    wait(qs.at[1, 1:16], ar_s.at[1, 1])
    wait(cs, c_s.at[0])
    for it in range(2):
        wait(psend.at[it], pair_s.at[it])
        wait(msg_s.at[it], rs_s.at[it, 0])
        wait(half_s.at[it], rs_s.at[it, 1])
        wait(msg_s.at[it], ag_s.at[it, 0])
        wait(half_s.at[it], ag_s.at[it, 1])
        wait(psend.at[it], sib_s.at[it])

    inv = inverse_factor(join_gram(1))
    factor_ref[...] = inv * math.sqrt(FEATURES)
    wait(cg.at[1:8], c_r.at[1])
    total = cg[z]
    for j in range(1, 8):
        total = total + cg[(z - j + 8) % 8]
    once = lax.broadcasted_iota(jnp.int32, (H, K), 1) < H
    form = jnp.concatenate([jnp.where(once, total[:, 0:K], 2.0 * total[:, 0:K]),
                            jnp.concatenate([jnp.zeros((H, H), F32), total[:, K:K + H]], axis=1)], axis=0)
    spread = dot_exact(inv, form) * inv
    captured = lax.dot_general(jnp.ones((8, K), F32), spread, (((1,), (1,)), ((), ())),
                               preferred_element_type=F32, precision=lax.Precision.HIGHEST)
    score_ref[...] = FEATURES * captured[0:1, :] / (total[0:1, K + H:K + H + 1] + 1e-6)
    wait(gg.at[1, 1:16], g_s.at[1])
    wait(cg.at[1:8], c_s.at[1])
    wait(x2_out, o_sem)


def on_device(differences, start_block):
    dma = pltpu.SemaphoreType.DMA
    pulled, factor, scores = pl.pallas_call(
        kernel,
        out_shape=(jax.ShapeDtypeStruct((K, WF), BF16), jax.ShapeDtypeStruct((K, K), F32),
                   jax.ShapeDtypeStruct((1, K), F32)),
        in_specs=[pl.BlockSpec(memory_space=pltpu.HBM), pl.BlockSpec(memory_space=pltpu.HBM)],
        out_specs=(pl.BlockSpec(memory_space=pltpu.HBM), pl.BlockSpec(memory_space=pltpu.VMEM),
                   pl.BlockSpec(memory_space=pltpu.VMEM)),
        scratch_shapes=[
            pltpu.VMEM((NP, WQ, PW), BF16),
            pltpu.VMEM((NP, K, PW), BF16),
            pltpu.VMEM((NP, K, PW), BF16),
            pltpu.VMEM((2, 8, K, PW), BF16),
            pltpu.VMEM((2, 8, K, PW), BF16),
            pltpu.VMEM((2, CHUNKS, 6, K, CW), BF16),
            pltpu.VMEM((2, CHUNKS, 6, K, CW), BF16),
            pltpu.VMEM((2, CHUNKS, 2, K, HALF), BF16),
            pltpu.VMEM((2, CHUNKS, 2, K, HALF), BF16),
            pltpu.VMEM((8, K, PW), F32),
            pltpu.VMEM((2, 16, ROWS, WQ), F32),
            pltpu.VMEM((2, 16, ROWS, WQ), F32),
            pltpu.VMEM((2, ROWS, WQ), F32),
            pltpu.VMEM((2, 16, ROWS, WQ), F32),
            pltpu.VMEM((4, K, WQ), F32),
            pltpu.VMEM((2, 16, K // 2, 128), F32),
            pltpu.VMEM((H, 128), F32),
            pltpu.VMEM((H, 128), F32),
            pltpu.VMEM((8, H, 128), F32),
            pltpu.VMEM((K, K), F32),
            pltpu.VMEM((8, 128), F32),
            dma((NP // LOAD,)), dma, dma,
            dma((2, 2)), dma((2, 2)),
            dma((2,)), dma((2, 5)),
            dma((2, 2)), dma((2, CHUNKS, 8)),
            dma((2, 2)), dma((2, CHUNKS, 8)),
            dma((2,)), dma((2, CHUNKS, 4)),
            dma((2,)), dma((2,)),
            dma((2,)), dma((2,)),
        ],
        compiler_params=pltpu.CompilerParams(collective_id=0, has_side_effects=True, vmem_limit_bytes=52 * 1024 * 1024),
    )(differences, start_block)
    directions = jnp.dot(factor, pulled.astype(F32), precision=lax.Precision.HIGH)
    return directions, scores


def solution(mesh):
    in_specs = (P("samp", "feat"), P(None, "feat"))
    out_specs = (P(None, "feat"), P("feat", None))
    return jax.shard_map(
        on_device, mesh=mesh, in_specs=in_specs, out_specs=out_specs, check_vma=False
    )
```

```python
import math

import jax
import jax.numpy as jnp
from jax import lax
from jax.experimental import pallas as pl
from jax.experimental.pallas import tpu as pltpu
from jax.sharding import PartitionSpec as P

FEATURES = 131072
K = 64
H = K // 2
NS = 576
WF = 8192
NP = 16
PW = WF // NP
CHUNKS = 2
CW = PW // CHUNKS
HALF = CW // 2
ROWS = K // 16
WQ = NS + K
LOAD = 1
MESH = pl.DeviceIdType.MESH
F32 = jnp.float32
BF16 = jnp.bfloat16


def dot_nn(a, b):
    return lax.dot_general(a, b, (((1,), (0,)), ((), ())), preferred_element_type=F32)


def dot_nt(a, b):
    return lax.dot_general(a, b, (((1,), (1,)), ((), ())), preferred_element_type=F32)


def dot_exact(a, b):
    return lax.dot_general(a, b, (((1,), (0,)), ((), ())), preferred_element_type=F32, precision=lax.Precision.HIGHEST)


def inverse_factor(gram):
    row = lax.broadcasted_iota(jnp.int32, (8, 2 * K), 0)
    col = lax.broadcasted_iota(jnp.int32, (8, 2 * K), 1)
    wide = jnp.concatenate([gram, jnp.zeros((K, K), F32)], axis=1)
    m = [wide[8 * g:8 * g + 8, :] + jnp.where(col == row + (K + 8 * g), 1.0, 0.0) for g in range(8)]
    out = []
    for b in range(8):
        cols = [[jnp.broadcast_to(m[g][:, 8 * b + k:8 * b + k + 1], (8, 2 * K)) for k in range(8)] for g in range(b, 8)]
        diag = jnp.zeros((8, 2 * K), F32)
        for k in range(8):
            d = cols[0][k][k:k + 1, :]
            r = 1.0 / d
            diag = jnp.where(row == k, d, diag)
            pivot_row = m[b][k:k + 1, :] * r
            factor = [jnp.where(row > k, cols[0][k], 0.0)] + [cols[i][k] for i in range(1, 8 - b)]
            for i in range(8 - b):
                m[b + i] = m[b + i] - factor[i] * pivot_row
            for kk in range(k + 1, 8):
                t = cols[0][k][kk:kk + 1, :] * r
                for i in range(8 - b):
                    cols[i][kk] = cols[i][kk] - factor[i] * t
        inv = lax.rsqrt(diag)
        inv = inv * (1.5 - 0.5 * ((diag * inv) * inv))
        out.append((m[b] * inv)[:, K:])
    return jnp.concatenate(out, axis=0)


def pack(square):
    return jnp.concatenate([square[0:K // 2], square[K // 2:]], axis=1)


def unpack(wide):
    return jnp.concatenate([wide[:, 0:K], wide[:, K:]], axis=0)


def ring_hops(d, n):
    return min(d, n - d)


PLANE = sorted([(dx, dy) for dx in range(4) for dy in range(4) if dx or dy],
               key=lambda o: -(ring_hops(o[0], 4) + ring_hops(o[1], 4)))
COLUMN = [4, 3, 5, 2, 6, 1, 7]


PAIRS = [4, 3, 5, 1, 7, 2, 6, 0]


def kernel(d_hbm, s_hbm, x2_out, factor_ref, score_ref,
           dv, sv, x2, psend, precv, msg_s, msg_r, half_s, half_r, acc,
           qs, qr, qo, qg, qf, gg, cs, cr, cg, g2, keep,
           d_sem, s_sem, o_sem, ar_s, ar_r, pair_s, pair_r, rs_s, rs_r,
           ag_s, ag_r, sib_s, sib_r, g_s, g_r, c_s, c_r):
    samp = lax.axis_index("samp")
    feat = lax.axis_index("feat")
    z = samp // 2
    c = samp % 2
    x = feat // 4
    y = feat % 4
    sibling = (z * 2 + (1 - c), feat)

    def chip(d):
        return (((z + d) % 8) * 2 + c, feat)

    def across(dx, dy):
        return ((x + dx) % 4) * 4 + (y + dy) % 4

    def send(src, dst, ssem, rsem, dev):
        pltpu.make_async_remote_copy(src_ref=src, dst_ref=dst, send_sem=ssem, recv_sem=rsem,
                                     device_id=dev, device_id_type=MESH).start()

    def wait(ref, sem):
        pltpu.make_async_copy(ref, ref, sem).wait()

    for p in range(NP):
        pltpu.make_async_copy(s_hbm.at[:, p * PW:(p + 1) * PW], sv.at[p], s_sem).start()
    for p in range(NP):
        pltpu.make_async_copy(d_hbm.at[:, p * PW:(p + 1) * PW], dv.at[p, 0:NS, :], d_sem.at[p // LOAD]).start()

    barrier = pltpu.get_barrier_semaphore()
    for dx, dy in PLANE:
        pl.semaphore_signal(barrier, inc=1, device_id=(samp, across(dx, dy)), device_id_type=MESH)
    for d in COLUMN:
        pl.semaphore_signal(barrier, inc=1, device_id=chip(d), device_id_type=MESH)
    pl.semaphore_signal(barrier, inc=1, device_id=sibling, device_id_type=MESH)

    def reduce_scatter_q(it, value):
        for j in range(16):
            qs[it, j] = value[j * ROWS:(j + 1) * ROWS, :]
        for dx, dy in PLANE:
            there = across(dx, dy)
            send(qs.at[it, there], qr.at[it, dx * 4 + dy], ar_s.at[it, 0], ar_r.at[it, 0], (samp, there))

    def gather_q(it):
        total = qs[it, feat]
        wait(qr.at[it, 1:16], ar_r.at[it, 0])
        for r in range(1, 16):
            total = total + qr[it, r]
        qo[it] = total
        qg[it, 0] = total
        for dx, dy in PLANE:
            send(qo.at[it], qg.at[it, dx * 4 + dy], ar_s.at[it, 1], ar_r.at[it, 1], (samp, across(dx, dy)))
        wait(qs.at[it, 1:16], ar_s.at[it, 0])

    def join_q(it):
        wait(qg.at[it, 1:16], ar_r.at[it, 1])
        for j in range(16):
            slot = ((x - j // 4 + 4) % 4) * 4 + (y - j % 4 + 4) % 4
            qf[2 + it, j * ROWS:(j + 1) * ROWS, :] = qg[it, slot]
        return qf[2 + it, :, 0:NS]

    def exchange_gram(it, gram):
        gg[it, 0] = pack(gram)
        for dx, dy in PLANE:
            send(gg.at[it, 0], gg.at[it, dx * 4 + dy], g_s.at[it], g_r.at[it], (samp, across(dx, dy)))

    def join_gram(it):
        wait(gg.at[it, 1:16], g_r.at[it])
        total = gg[it, 0]
        for j in range(1, 16):
            total = total + gg[it, j]
        return unpack(total)

    q = jnp.zeros((K, NS), F32)
    wait(sv, s_sem)
    for p in range(NP):
        if p % LOAD == 0:
            wait(dv.at[p:p + LOAD, 0:NS, :], d_sem.at[p // LOAD])
        q = q + dot_nt(sv[p], dv[p, 0:NS, :])
    pl.semaphore_wait(barrier, 23)
    reduce_scatter_q(0, jnp.concatenate([q, jnp.zeros((K, K), F32)], axis=1))

    def energy_step(p, total):
        wide = dv[p, 0:NS, :].astype(F32)
        return total + jnp.sum(wide * wide, axis=0, keepdims=True)

    energy = lax.fori_loop(0, NP, energy_step, jnp.zeros((1, PW), F32))
    keep[...] = jnp.broadcast_to(jnp.sum(energy, axis=1, keepdims=True), (8, 128))
    gather_q(0)
    projected = join_q(0).astype(BF16)

    def pull_and_scatter(it, projected):
        def theirs(*ds):
            for d in ds:
                k = PAIRS.index(d)
                psend[it, k] = dot_nn(projected, dv[(1 - c) * 8 + (z + d) % 8, 0:NS, :]).astype(BF16)
                send(psend.at[it, k], precv.at[it, k], pair_s.at[it], pair_r.at[it, (k + 1) // 2], sibling)

        def ours(*ds):
            for d in ds:
                acc[d] = dot_nn(projected, dv[c * 8 + (z + d) % 8, 0:NS, :])

        def join(group):
            first, last = ((0, 1), (1, 3), (3, 5), (5, 7), (7, 8))[group]
            wait(precv.at[it, first:last], pair_r.at[it, group])

        def both(d):
            return acc[d] + precv[it, PAIRS.index(d)].astype(F32)

        def post(slot, ch, value, dev):
            msg_s[it, ch, slot] = value.astype(BF16)
            send(msg_s.at[it, ch, slot], msg_r.at[it, ch, slot], rs_s.at[it, 0], rs_r.at[it, ch, slot], dev)

        def post_half(slot, ch, value, dev):
            half_s[it, ch, slot] = value.astype(BF16)
            send(half_s.at[it, ch, slot], half_r.at[it, ch, slot], rs_s.at[it, 1], rs_r.at[it, ch, 6 + slot], dev)

        def arrived(slot, ch):
            wait(msg_r.at[it, ch, slot] if slot < 6 else half_r.at[it, ch, slot - 6], rs_r.at[it, ch, slot])

        def cols(ch):
            return slice(ch * CW, (ch + 1) * CW)

        theirs(4, 3, 5)
        ours(4, 3, 5)
        theirs(1, 7)
        join(0)
        part4 = both(4)
        for ch in range(CHUNKS):
            part = part4[:, cols(ch)]
            post_half(0, ch, part[:, 0:HALF], chip(2))
            post_half(1, ch, part[:, HALF:], chip(6))
        join(1)
        part3, part5 = both(3), both(5)
        for ch in range(CHUNKS):
            post(0, ch, part3[:, cols(ch)], chip(1))
            post(1, ch, part5[:, cols(ch)], chip(7))
        ours(1, 7)
        theirs(2, 6, 0)
        join(2)
        part1, part7 = both(1), both(7)
        for ch in range(CHUNKS):
            post(2, ch, part1[:, cols(ch)], chip(1))
            post(3, ch, part7[:, cols(ch)], chip(7))
        ours(2, 6, 0)
        join(3)
        acc[2] = both(2)
        acc[6] = both(6)
        for ch in range(CHUNKS):
            arrived(0, ch)
            arrived(6, ch)
            part = acc[2, :, cols(ch)] + msg_r[it, ch, 0].astype(F32)
            half = half_r[it, ch, 0].astype(F32)
            post(4, ch, jnp.concatenate([part[:, 0:HALF] + half, part[:, HALF:]], axis=1), chip(2))
            arrived(1, ch)
            arrived(7, ch)
            part = acc[6, :, cols(ch)] + msg_r[it, ch, 1].astype(F32)
            half = half_r[it, ch, 1].astype(F32)
            post(5, ch, jnp.concatenate([part[:, 0:HALF], part[:, HALF:] + half], axis=1), chip(6))
        join(4)
        acc[0] = both(0)
        for ch in range(CHUNKS):
            arrived(2, ch)
            arrived(3, ch)
            part = acc[0, :, cols(ch)] + msg_r[it, ch, 2].astype(F32) + msg_r[it, ch, 3].astype(F32)
            arrived(4, ch)
            arrived(5, ch)
            yield (part + msg_r[it, ch, 4].astype(F32) + msg_r[it, ch, 5].astype(F32)).astype(BF16)

    def gather(it, slot, pieces, use):
        here = c * 8
        there = (1 - c) * 8

        def pass_on(k, ch, d, dev, start=0, width=CW):
            ref = slot(here + (z + d) % 8, slice(ch * CW + start, ch * CW + start + width))
            send(ref, ref, ag_s.at[it, 1 if k in (4, 5) else 0], ag_r.at[it, ch, k], dev)

        def arrived(ch, k):
            wait(half_r.at[it, ch, 0] if k in (4, 5) else msg_r.at[it, ch, 0], ag_r.at[it, ch, k])

        def to_sibling(ch, d):
            ref = slot(here + (z + d) % 8, slice(ch * CW, (ch + 1) * CW))
            group = {0: 0, 6: 1, 2: 1, 7: 2, 1: 2, 5: 3, 3: 3, 4: 3}[d]
            send(ref, ref, sib_s.at[it], sib_r.at[it, ch, group], sibling)

        def use_own(ch, *ds):
            use([here + (z + d) % 8 for d in ds], slice(ch * CW, (ch + 1) * CW))

        def use_sibling(ch, *ds):
            group = {0: 0, 6: 1, 7: 2, 5: 3}[ds[0]]
            wait(msg_r.at[it, ch, 0:len(ds)], sib_r.at[it, ch, group])
            use([there + (z + d) % 8 for d in ds], slice(ch * CW, (ch + 1) * CW))

        for ch, piece in enumerate(pieces):
            slot(here + z, slice(ch * CW, (ch + 1) * CW))[...] = piece
            pass_on(0, ch, 0, chip(2))
            pass_on(1, ch, 0, chip(6))
            to_sibling(ch, 0)
        for ch in range(CHUNKS):
            pass_on(2, ch, 0, chip(1))
            pass_on(3, ch, 0, chip(7))
        use_own(0, 0)
        use_own(1, 0)
        use_sibling(0, 0)
        use_sibling(1, 0)
        for ch in range(CHUNKS):
            arrived(ch, 0)
            pass_on(4, ch, 6, chip(2), 0, HALF)
            pass_on(6, ch, 6, chip(1))
            to_sibling(ch, 6)
            arrived(ch, 1)
            pass_on(5, ch, 2, chip(6), HALF, HALF)
            pass_on(7, ch, 2, chip(7))
            to_sibling(ch, 2)
            use_own(ch, 6, 2)
        for ch in range(CHUNKS):
            arrived(ch, 2)
            to_sibling(ch, 7)
            arrived(ch, 3)
            to_sibling(ch, 1)
            use_own(ch, 7, 1)
            use_sibling(ch, 6, 2)
        use_sibling(0, 7, 1)
        use_sibling(1, 7, 1)
        for ch in range(CHUNKS):
            arrived(ch, 6)
            to_sibling(ch, 5)
            arrived(ch, 7)
            to_sibling(ch, 3)
            arrived(ch, 4)
            arrived(ch, 5)
            to_sibling(ch, 4)
            use_own(ch, 5, 3, 4)
        for ch in range(CHUNKS):
            use_sibling(ch, 5, 3, 4)

    qf[0] = jnp.zeros((K, WQ), F32)

    def use_first(ps, cols):
        qf[0] += sum(dot_nt(dv[p, NS:, cols], dv[p, :, cols]) for p in ps)

    gather(0, lambda p, cols: dv.at[p, NS:, cols], pull_and_scatter(0, projected), use_first)
    reduce_scatter_q(1, qf[0])
    exchange_gram(0, qf[0, :, NS:])
    gather_q(1)
    inv = inverse_factor(join_gram(0))
    projected = dot_exact(inv, join_q(1)).astype(BF16)

    qf[1] = jnp.zeros((K, WQ), F32)

    g2[...] = jnp.zeros((K, K), F32)

    def use_second(ps, cols):
        qf[1, :, 0:NS] += sum(dot_nt(x2[p, :, cols], dv[p, 0:NS, cols]) for p in ps)
        g2[...] += sum(dot_nt(x2[p, :, cols], x2[p, :, cols]) for p in ps)

    gather(1, lambda p, cols: x2.at[p, :, cols], pull_and_scatter(1, projected), use_second)
    exchange_gram(1, g2[...])
    for p in range(NP):
        pltpu.make_async_copy(x2.at[p], x2_out.at[:, p * PW:(p + 1) * PW], o_sem).start()

    along = qf[1, :, 0:NS]
    high = along.astype(BF16)
    rest = along - high.astype(F32)
    middle = rest.astype(BF16)
    low = (rest - middle.astype(F32)).astype(BF16)
    parts = jnp.concatenate([high, middle, low], axis=0)
    nine = dot_nt(parts, parts)
    rows = nine[0:K] + nine[K:2 * K] + nine[2 * K:]
    square = rows[:, 0:K] + rows[:, K:2 * K] + rows[:, 2 * K:]
    cs[...] = jnp.concatenate([square[0:H, :], square[H:, H:], jnp.broadcast_to(keep[0:1, 0:H], (H, H))], axis=1)
    send(cs, cr, c_s.at[0], c_r.at[0], sibling)
    wait(cr, c_r.at[0])
    cg[0] = cs[...] + cr[...]
    for d in COLUMN:
        send(cg.at[0], cg.at[d], c_s.at[1], c_r.at[1], chip(d))

    wait(gg.at[0, 1:16], g_s.at[0])
    wait(qs.at[1, 1:16], ar_s.at[0, 1])
    wait(qs.at[1, 1:16], ar_s.at[1, 1])
    wait(cs, c_s.at[0])
    for it in range(2):
        wait(psend.at[it], pair_s.at[it])
        wait(msg_s.at[it], rs_s.at[it, 0])
        wait(half_s.at[it], rs_s.at[it, 1])
        wait(msg_s.at[it], ag_s.at[it, 0])
        wait(half_s.at[it], ag_s.at[it, 1])
        wait(psend.at[it], sib_s.at[it])

    inv = inverse_factor(join_gram(1))
    factor_ref[...] = inv * math.sqrt(FEATURES)
    wait(cg.at[1:8], c_r.at[1])
    total = cg[z]
    for j in range(1, 8):
        total = total + cg[(z - j + 8) % 8]
    once = lax.broadcasted_iota(jnp.int32, (H, K), 1) < H
    form = jnp.concatenate([jnp.where(once, total[:, 0:K], 2.0 * total[:, 0:K]),
                            jnp.concatenate([jnp.zeros((H, H), F32), total[:, K:K + H]], axis=1)], axis=0)
    spread = dot_exact(inv, form) * inv
    captured = lax.dot_general(jnp.ones((8, K), F32), spread, (((1,), (1,)), ((), ())),
                               preferred_element_type=F32, precision=lax.Precision.HIGHEST)
    score_ref[...] = FEATURES * captured[0:1, :] / (total[0:1, K + H:K + H + 1] + 1e-6)
    wait(gg.at[1, 1:16], g_s.at[1])
    wait(cg.at[1:8], c_s.at[1])
    wait(x2_out, o_sem)


def on_device(differences, start_block):
    dma = pltpu.SemaphoreType.DMA
    pulled, factor, scores = pl.pallas_call(
        kernel,
        out_shape=(jax.ShapeDtypeStruct((K, WF), BF16), jax.ShapeDtypeStruct((K, K), F32),
                   jax.ShapeDtypeStruct((1, K), F32)),
        in_specs=[pl.BlockSpec(memory_space=pltpu.HBM), pl.BlockSpec(memory_space=pltpu.HBM)],
        out_specs=(pl.BlockSpec(memory_space=pltpu.HBM), pl.BlockSpec(memory_space=pltpu.VMEM),
                   pl.BlockSpec(memory_space=pltpu.VMEM)),
        scratch_shapes=[
            pltpu.VMEM((NP, WQ, PW), BF16),
            pltpu.VMEM((NP, K, PW), BF16),
            pltpu.VMEM((NP, K, PW), BF16),
            pltpu.VMEM((2, 8, K, PW), BF16),
            pltpu.VMEM((2, 8, K, PW), BF16),
            pltpu.VMEM((2, CHUNKS, 6, K, CW), BF16),
            pltpu.VMEM((2, CHUNKS, 6, K, CW), BF16),
            pltpu.VMEM((2, CHUNKS, 2, K, HALF), BF16),
            pltpu.VMEM((2, CHUNKS, 2, K, HALF), BF16),
            pltpu.VMEM((8, K, PW), F32),
            pltpu.VMEM((2, 16, ROWS, WQ), F32),
            pltpu.VMEM((2, 16, ROWS, WQ), F32),
            pltpu.VMEM((2, ROWS, WQ), F32),
            pltpu.VMEM((2, 16, ROWS, WQ), F32),
            pltpu.VMEM((4, K, WQ), F32),
            pltpu.VMEM((2, 16, K // 2, 128), F32),
            pltpu.VMEM((H, 128), F32),
            pltpu.VMEM((H, 128), F32),
            pltpu.VMEM((8, H, 128), F32),
            pltpu.VMEM((K, K), F32),
            pltpu.VMEM((8, 128), F32),
            dma((NP // LOAD,)), dma, dma,
            dma((2, 2)), dma((2, 2)),
            dma((2,)), dma((2, 5)),
            dma((2, 2)), dma((2, CHUNKS, 8)),
            dma((2, 2)), dma((2, CHUNKS, 8)),
            dma((2,)), dma((2, CHUNKS, 4)),
            dma((2,)), dma((2,)),
            dma((2,)), dma((2,)),
        ],
        compiler_params=pltpu.CompilerParams(collective_id=0, has_side_effects=True, vmem_limit_bytes=52 * 1024 * 1024),
    )(differences, start_block)
    directions = jnp.dot(factor, pulled.astype(F32), precision=lax.Precision.HIGH)
    return directions, scores


def solution(mesh):
    in_specs = (P("samp", "feat"), P(None, "feat"))
    out_specs = (P(None, "feat"), P("feat", None))
    return jax.shard_map(
        on_device, mesh=mesh, in_specs=in_specs, out_specs=out_specs, check_vma=False
    )
```
